128 devices in a mesh: expert: 32 (over y, x_hi, z), tensor: 4 (over x_lo, core).
Axes of the slice: x: 4 (x_hi: 2, x_lo: 2; x = x_hi * 2 + x_lo), y: 4, z: 4, core: 2. Of those that a mesh axis runs over, the one named last changes fastest.
Arguments:
- hidden_in: bfloat16 [16384, 4096], P(('expert', 'tensor')), may hold values from -20 to 20
- context: bfloat16 [16384, 4096], P('expert', 'tensor'), may hold values from -6 to 6
- w_out: bfloat16 [4096, 4096], P('tensor', 'expert'), may hold values from -0.09375 to 0.09375
- norm_gain: float32 [4096], replicated, may hold values from 0.25 to 1.75
- expert_ids: int32 [16384, 8], P(('expert', 'tensor')), may hold values from 0 to 127, all different within a row; in each aligned block of 128 rows (0 to 127, 128 to 255, ...) at most 9 rows name the same one
- route_weight: float32 [16384, 8], P(('expert', 'tensor')), may hold values from 0.05 to 1
- w_gate_up: bfloat16 [128, 4096, 1536], P(('expert', 'tensor')), may hold values from -0.09375 to 0.09375
- w_down: bfloat16 [128, 768, 4096], P(('expert', 'tensor')), may hold values from -0.21875 to 0.21875
Outputs:
- attended: bfloat16 [16384, 4096], P(('expert', 'tensor'))
- mixed: bfloat16 [16384, 4096], P(('expert', 'tensor'))
The draws below stay inside these ranges and needn't reach their ends.
Inputs may be any that keep to these rules, and one draw needn't show every extreme that they name: `expert_ids`: each row names 8 different experts. Among the 128 rows of one device no expert is named more than 9 times, and in every draw some expert is named exactly 9 times by the rows of some device.
All inputs are finite; a program needn't handle non-finite values.
Results may differ from the reference program's by a relative error of at most 0.0053.
Values may be sent and summed in bfloat16 or wider, within the bound.
A program may use at most 128 MiB of HBM per device.

```python
import math
import jax
import jax.numpy as jnp
import numpy as np
from jax import lax

D = 4096
HQ = 32
HD = 128
FF = 768
TOP_K = 8
TOK_DEV = 128
EXPERTS = 128
CAPACITY = 9
TOKENS = 16384
N_EXPERT = 32
N_TENSOR = 4


def draw_hidden_in(key, part):
    row_key, column_key, value_key = jax.random.split(key, 3)
    row_scale = jnp.exp(jax.random.uniform(row_key, (TOKENS, 1), jnp.float32) * math.log(10.0))
    column_scale = jnp.exp(jax.random.uniform(column_key, (1, D), jnp.float32) * math.log(10.0))
    values = jnp.clip(jax.random.normal(value_key, (TOKENS, D), jnp.float32), -4.0, 4.0)
    return (0.05 * values * row_scale * column_scale).astype(jnp.bfloat16)


def block_levels(rng, dims, cuts, smallest, largest):
    level = 1.0
    for position, parts in cuts:
        draws = jax.random.uniform(jax.random.fold_in(jax.random.fold_in(rng, 6), position), (parts,), jnp.float32, smallest / len(cuts), largest / len(cuts))
        level = level * jnp.repeat(jnp.exp(draws), dims[position] // parts).reshape((-1,) + (1,) * (len(dims) - 1 - position))
    return level


def deal_out(stream_key, own, number, rows, number_of, top, most, skew):
    ranking = jax.random.permutation(stream_key, number_of)
    crowded, usual = shares(number_of, rows * top, most, skew, True), shares(number_of, rows * top, most, skew, False)
    places = jnp.arange(number_of)

    def named(sizes, rotation):
        used = int((sizes > 0).sum())
        fixed = max(1, used // 4)
        moved = fixed + (places - fixed + rotation * (used - fixed)) % max(1, number_of - fixed)
        return jnp.zeros((number_of,), jnp.int32).at[ranking[jnp.where(places < fixed, places, moved)]].set(jnp.asarray(sizes, jnp.int32))

    sizes = jnp.where(number % 4 == 0, named(crowded, number // 4), named(usual, number - number // 4 - 1))
    mixed = jax.random.permutation(jax.random.fold_in(own, 3), number_of)
    giver, receiver = mixed[0:number_of // 2 * 2:2], mixed[1:number_of // 2 * 2:2]
    room = jnp.minimum(sizes[giver] - 1, most - sizes[receiver]) // 2
    room = jnp.where((giver == ranking[0]) | (receiver == ranking[0]) | (sizes[receiver] == 0), 0, jnp.maximum(room, 0))
    moved = jax.random.randint(jax.random.fold_in(own, 4), (number_of // 2,), 0, 1 << 20) % (room + 1)
    sizes = sizes.at[giver].add(-moved).at[receiver].add(moved)
    members = jnp.searchsorted(jnp.cumsum(sizes), jnp.arange(rows * top), side="right").astype(jnp.int32)
    table = members.reshape(top, rows).T
    table = table[jax.random.permutation(jax.random.fold_in(own, 1), rows)]
    rotation = jax.random.randint(jax.random.fold_in(own, 2), (rows, 1), 0, top)
    return jnp.take_along_axis(table, (jnp.arange(top)[None, :] + rotation) % top, axis=1)


def shares(count, total, reach, lean, full):
    weights = [(1 << 20) // math.isqrt(standing ** lean) + 1 for standing in range(1, count + 1)]
    largest = reach if full else min(reach, max(-(-total // count), total * weights[0] // sum(weights)))
    least = 1 if total - largest >= count - 1 else 0
    given, rest = [largest] + [least] * (count - 1), total - largest - least * (count - 1)
    while rest > 0:
        movable = [i for i in range(1, count) if given[i] < largest] or [i for i in range(1, count) if given[i] < reach]
        whole, left = sum([weights[i] for i in movable]), rest
        for i in movable:
            more = min(reach - given[i], max(1, left * weights[i] // whole), rest)
            given[i] = given[i] + more
            rest = rest - more
    return np.array(given)


def normal_values(stream_key, shape, scale, most, cuts=(), kind=jnp.bfloat16):
    array = jax.random.normal(stream_key, shape, jnp.float32) * scale
    if len(cuts) > 0:
        array = block_levels(stream_key, shape, cuts, -0.22, 0.18) * array
    return jnp.clip(array, min=-most, max=most).astype(kind)


def setup_inputs(seed: int = 0) -> dict:
    keys = jax.random.split(jax.random.key(seed), 9)
    hidden_in = draw_hidden_in(jax.random.fold_in(keys[8], 71), 0)
    context = normal_values(keys[1], (TOKENS, HQ * HD), 1.0, 6.0, ((0, 32), (1, 4)))
    w_out = normal_values(keys[2], (HQ * HD, D), (HQ * HD) ** -0.5, 0.09375, ((0, 4), (1, 32)))
    norm_gain = jnp.clip(1.0 + 0.15 * jax.random.normal(keys[3], (D,), jnp.float32), 0.25, 1.75)
    expert_ids_keys = jax.random.split(jax.random.fold_in(keys[4], 1), TOKENS // TOK_DEV)
    expert_ids_turns = jax.random.permutation(jax.random.fold_in(keys[4], 3), TOKENS // TOK_DEV)
    expert_ids = jax.vmap(lambda own, number: deal_out(jax.random.fold_in(keys[4], 2), own, number, TOK_DEV, EXPERTS, TOP_K, CAPACITY, 2))(expert_ids_keys, expert_ids_turns).reshape((TOKENS, TOP_K))
    route_weight = jnp.clip(jnp.exp(math.log(1.0) - 2.9957323 * jax.random.uniform(keys[5], (TOKENS, TOP_K), jnp.float32) ** block_levels(keys[5], (TOKENS, TOP_K), ((0, 128),), -0.2, 0.2)), 0.05, 1.0)
    w_gate_up = normal_values(keys[6], (EXPERTS, D, 2 * FF), D ** -0.5, 0.09375, ((0, 128),))
    w_down = normal_values(keys[7], (EXPERTS, FF, D), FF ** -0.5, 0.21875, ((0, 128),))
    return dict(hidden_in=hidden_in, context=context, w_out=w_out, norm_gain=norm_gain, expert_ids=expert_ids, route_weight=route_weight, w_gate_up=w_gate_up, w_down=w_down)


def slot_positions(expert_ids, devices):
    chosen = expert_ids.reshape(devices, -1)
    onehot = (chosen[:, :, None] == jnp.arange(EXPERTS, dtype=jnp.int32)[None, None, :]).astype(jnp.int32)
    before = jnp.cumsum(onehot, axis=1) - onehot
    return (chosen, lax.optimization_barrier(jnp.sum(before * onehot, axis=2)).astype(jnp.int32))

def reference(hidden_in, context, w_out, norm_gain, expert_ids, route_weight, w_gate_up, w_down):
    projected = jnp.dot(context, w_out, preferred_element_type=jnp.float32)
    residual = hidden_in.astype(jnp.float32) + projected
    attended = residual.astype(jnp.bfloat16)
    inverse = lax.rsqrt(lax.optimization_barrier(jnp.mean(residual * residual, axis=1, keepdims=True)) + 1e-06)
    normed = (residual * inverse * norm_gain[None, :]).astype(jnp.bfloat16)
    devices = N_EXPERT * N_TENSOR
    chosen, slots = slot_positions(expert_ids, devices)
    device_of = jnp.broadcast_to(jnp.arange(devices, dtype=jnp.int32)[:, None], chosen.shape)
    token_of = jnp.broadcast_to(jnp.arange(TOKENS, dtype=jnp.int32)[:, None], (TOKENS, TOP_K)).reshape(devices, -1)
    table = jnp.full((EXPERTS, devices, CAPACITY), TOKENS, jnp.int32).at[chosen, device_of, slots].set(token_of)
    weights = jnp.zeros((EXPERTS, devices, CAPACITY), jnp.float32).at[chosen, device_of, slots].set(route_weight.reshape(devices, -1))

    def one_expert(carry, inputs):
        token_index, row_weight, gate_up, down_proj = inputs
        gathered = jnp.take(normed, token_index, axis=0, mode='fill', fill_value=0)
        gate_and_up = jnp.dot(gathered, gate_up, preferred_element_type=jnp.float32)
        activated = (jax.nn.silu(gate_and_up[:, :FF]) * gate_and_up[:, FF:]).astype(jnp.bfloat16)
        result = jnp.dot(activated, down_proj, preferred_element_type=jnp.float32).astype(jnp.bfloat16)
        carry = carry.at[token_index].add(row_weight[:, None] * result.astype(jnp.float32), mode='drop')
        return (carry, None)
    moe_sum, _ = lax.scan(one_expert, jnp.zeros((TOKENS, D), jnp.float32), (table.reshape(EXPERTS, -1), weights.reshape(EXPERTS, -1), w_gate_up, w_down))
    mixed = (residual + moe_sum).astype(jnp.bfloat16)
    return (attended, mixed)
```

```python
import jax
import jax.numpy as jnp
from jax import lax
from jax.sharding import PartitionSpec as P

LANES = 128


def expert_block(received, w_gate_up, w_down):
    hidden_units = w_down.shape[1]
    gate_and_up = jnp.dot(received, w_gate_up[0], preferred_element_type=jnp.float32)
    activated = (jax.nn.silu(gate_and_up[:, :hidden_units]) * gate_and_up[:, hidden_units:]).astype(
        jnp.bfloat16
    )
    return jnp.dot(activated, w_down[0], preferred_element_type=jnp.float32).astype(jnp.bfloat16)


def split_bf16(x):
    hi = x.astype(jnp.bfloat16)
    rest = x - hi.astype(jnp.float32)
    mid = rest.astype(jnp.bfloat16)
    lo = (rest - mid.astype(jnp.float32)).astype(jnp.bfloat16)
    return hi, mid, lo


def on_device(hidden_in, context, w_out, norm_gain, expert_ids, route_weight, w_gate_up, w_down):
    tok_count, width = hidden_in.shape
    chunks = width // LANES
    partial_sums = jnp.dot(
        context,
        lax.all_gather(w_out, "expert", axis=1, tiled=True),
        preferred_element_type=jnp.float32,
    )
    projected = lax.psum_scatter(partial_sums, "tensor", scatter_dimension=0, tiled=True)
    residual = hidden_in.astype(jnp.float32) + projected
    attended = residual.astype(jnp.bfloat16)
    inverse = lax.rsqrt(jnp.mean(residual * residual, axis=1, keepdims=True) + 1e-06)
    normed = (residual * inverse * norm_gain[None, :]).astype(jnp.bfloat16)
    top_count = expert_ids.shape[1]
    expert_count = lax.axis_size("expert")
    tensor_count = lax.axis_size("tensor")
    experts_all = expert_count * tensor_count
    capacity = tok_count * top_count * 9 // (8 * experts_all)
    rows_all = experts_all * capacity
    chosen = expert_ids.reshape(-1)
    onehot = (chosen[:, None] == jnp.arange(experts_all, dtype=jnp.int32)[None, :]).astype(
        jnp.int32
    )
    before = jnp.cumsum(onehot, axis=0) - onehot
    slots = jnp.sum(before * onehot, axis=1)
    target = (chosen * capacity + slots).reshape(tok_count, top_count)
    place = jnp.arange(rows_all, dtype=jnp.int32)[:, None, None] == target[None, :, :]
    dispatch = jnp.any(place, axis=2).astype(jnp.bfloat16)
    normed3 = normed.reshape(tok_count, chunks, LANES)
    send = jnp.einsum(
        "ri,icl->rcl", dispatch, normed3, preferred_element_type=jnp.float32
    ).astype(jnp.bfloat16)
    send = send.reshape(experts_all, capacity * chunks, LANES)
    received = lax.all_to_all(send, ("expert", "tensor"), split_axis=0, concat_axis=0, tiled=True)
    outputs = expert_block(received.reshape(rows_all, width), w_gate_up, w_down)
    outputs = outputs.reshape(experts_all, capacity * chunks, LANES)
    returned = lax.all_to_all(
        outputs, ("expert", "tensor"), split_axis=0, concat_axis=0, tiled=True
    )
    returned = returned.reshape(rows_all, chunks, LANES)
    combine = jnp.sum(
        jnp.where(place, route_weight[None, :, :], 0.0), axis=2
    ).T
    hi, mid, lo = split_bf16(combine)
    stacked = jnp.concatenate([hi, mid, lo], axis=0)
    parts = jnp.einsum("ir,rcl->icl", stacked, returned, preferred_element_type=jnp.float32)
    moe_sum = (parts[:tok_count] + parts[tok_count : 2 * tok_count]) + parts[2 * tok_count :]
    mixed = (residual + moe_sum.reshape(tok_count, width)).astype(jnp.bfloat16)
    return (attended, mixed)


def solution(mesh):
    in_specs = (
        P(("expert", "tensor"), None),
        P("expert", "tensor"),
        P("tensor", "expert"),
        P(),
        P(("expert", "tensor"), None),
        P(("expert", "tensor"), None),
        P(("expert", "tensor"), None, None),
        P(("expert", "tensor"), None, None),
    )
    out_specs = (P(("expert", "tensor"), None), P(("expert", "tensor"), None))
    return jax.shard_map(
        on_device, mesh=mesh, in_specs=in_specs, out_specs=out_specs, check_vma=False
    )
```

```python
import jax
import jax.numpy as jnp
import numpy as np
from jax import lax
from jax.sharding import Mesh
from jax.sharding import PartitionSpec as P

LANES = 128
ALL = ("expert", "xlo", "core")


def expert_block(received, w_gate_up, w_down):
    hidden_units = w_down.shape[1]
    gate_and_up = jnp.dot(received, w_gate_up[0], preferred_element_type=jnp.float32)
    activated = (jax.nn.silu(gate_and_up[:, :hidden_units]) * gate_and_up[:, hidden_units:]).astype(
        jnp.bfloat16
    )
    return jnp.dot(activated, w_down[0], preferred_element_type=jnp.float32).astype(jnp.bfloat16)


def project(context, w_out):
    n_x = lax.axis_size("xlo")
    n_c = lax.axis_size("core")
    rows = context.shape[0] // (n_x * n_c)
    context = context.reshape(n_x, n_c, rows, -1).transpose(1, 0, 2, 3).reshape(n_x * n_c * rows, -1)
    partial_sums = jnp.dot(
        context,
        lax.all_gather(w_out, "expert", axis=1, tiled=True),
        preferred_element_type=jnp.float32,
    )
    width = partial_sums.shape[1]
    chip_sums = lax.psum_scatter(partial_sums, "core", scatter_dimension=0, tiled=True)
    chip_sums = chip_sums.reshape(n_x, rows, width)
    me = lax.axis_index("xlo")
    own = lax.dynamic_index_in_dim(chip_sums, me, axis=0, keepdims=False)
    other = lax.dynamic_index_in_dim(chip_sums, 1 - me, axis=0, keepdims=False)
    arrived = lax.ppermute(other.astype(jnp.bfloat16), "xlo", perm=[(0, 1), (1, 0)])
    return own + arrived.astype(jnp.float32)


def on_device(hidden_in, context, w_out, norm_gain, expert_ids, route_weight, w_gate_up, w_down):
    tok_count, width = hidden_in.shape
    chunks = width // LANES
    projected = project(context, w_out)
    residual = hidden_in.astype(jnp.float32) + projected
    attended = residual.astype(jnp.bfloat16)
    inverse = lax.rsqrt(jnp.mean(residual * residual, axis=1, keepdims=True) + 1e-06)
    normed = (residual * inverse * norm_gain[None, :]).astype(jnp.bfloat16)
    top_count = expert_ids.shape[1]
    experts_all = lax.axis_size(ALL)
    capacity = tok_count * top_count * 9 // (8 * experts_all)
    rows_all = experts_all * capacity
    chosen = expert_ids.reshape(-1)
    onehot = (chosen[:, None] == jnp.arange(experts_all, dtype=jnp.int32)[None, :]).astype(
        jnp.int32
    )
    before = jnp.cumsum(onehot, axis=0) - onehot
    slots = jnp.sum(before * onehot, axis=1)
    target = chosen * capacity + slots
    token_index = jnp.arange(tok_count * top_count, dtype=jnp.int32) // top_count
    source = jnp.full((rows_all,), tok_count, jnp.int32).at[target].set(token_index)
    normed3 = jnp.concatenate(
        [normed.reshape(tok_count, chunks, LANES), jnp.zeros((1, chunks, LANES), jnp.bfloat16)],
        axis=0,
    )
    send = jnp.take(normed3, source, axis=0)
    send = send.reshape(experts_all, capacity * chunks, LANES)
    received = lax.all_to_all(send, ALL, split_axis=0, concat_axis=0, tiled=True)
    outputs = expert_block(received.reshape(rows_all, width), w_gate_up, w_down)
    outputs = outputs.reshape(experts_all, capacity * chunks, LANES)
    returned = lax.all_to_all(outputs, ALL, split_axis=0, concat_axis=0, tiled=True)
    returned = returned.reshape(rows_all, chunks, LANES)
    picked = jnp.take(returned, target, axis=0).reshape(tok_count, top_count, chunks, LANES)
    moe_sum = jnp.sum(route_weight[:, :, None, None] * picked.astype(jnp.float32), axis=1)
    mixed = (residual + moe_sum.reshape(tok_count, width)).astype(jnp.bfloat16)
    return (attended, mixed)


def solution(mesh):
    n_expert = mesh.shape["expert"]
    n_tensor = mesh.shape["tensor"]
    n_core = 2 if n_tensor % 2 == 0 else 1
    devices = np.asarray(mesh.devices).reshape(n_expert, n_tensor // n_core, n_core)
    mesh3 = Mesh(devices, ALL)
    tensor = ("xlo", "core")
    in_specs = (
        P(ALL, None),
        P("expert", tensor),
        P(tensor, "expert"),
        P(),
        P(ALL, None),
        P(ALL, None),
        P(ALL, None, None),
        P(ALL, None, None),
    )
    out_specs = (P(ALL, None), P(ALL, None))
    return jax.shard_map(
        on_device, mesh=mesh3, in_specs=in_specs, out_specs=out_specs, check_vma=False
    )
```

```python
import jax
import jax.numpy as jnp
import numpy as np
from jax import lax
from jax.experimental import pallas as pl
from jax.experimental.pallas import tpu as pltpu
from jax.sharding import Mesh
from jax.sharding import PartitionSpec as P

LANES = 128
ALL = ("expert", "xlo", "core")


def expert_block(received, w_gate_up, w_down):
    hidden_units = w_down.shape[1]
    gate_and_up = jnp.dot(received, w_gate_up[0], preferred_element_type=jnp.float32)
    activated = (jax.nn.silu(gate_and_up[:, :hidden_units]) * gate_and_up[:, hidden_units:]).astype(
        jnp.bfloat16
    )
    return jnp.dot(activated, w_down[0], preferred_element_type=jnp.float32).astype(jnp.bfloat16)


def gather_kernel(n, w_ref, out_ref, send_sem, recv_sem, local_sem):
    me = lax.axis_index("expert")
    cols = w_ref.shape[1]
    barrier = pltpu.get_barrier_semaphore()
    for step in range(1, n):
        pl.semaphore_signal(
            barrier, inc=1, device_id={"expert": lax.rem(me + step, n)},
            device_id_type=pl.DeviceIdType.MESH,
        )
    pl.semaphore_wait(barrier, n - 1)
    mine = out_ref.at[:, pl.ds(pl.multiple_of(me * cols, cols), cols)]
    local = pltpu.make_async_copy(w_ref, mine, local_sem)
    local.start()
    copies = []
    for step in range(1, n):
        copy = pltpu.make_async_remote_copy(
            src_ref=w_ref,
            dst_ref=mine,
            send_sem=send_sem.at[step],
            recv_sem=recv_sem.at[me],
            device_id={"expert": lax.rem(me + step, n)},
            device_id_type=pl.DeviceIdType.MESH,
        )
        copy.start()
        copies.append(copy)
    local.wait()
    for step in range(1, n):
        copies[step - 1].wait_send()
        source = lax.rem(me + n - step, n)
        pltpu.make_async_remote_copy(
            src_ref=w_ref,
            dst_ref=out_ref.at[:, pl.ds(pl.multiple_of(source * cols, cols), cols)],
            send_sem=send_sem.at[step],
            recv_sem=recv_sem.at[source],
            device_id={"expert": source},
            device_id_type=pl.DeviceIdType.MESH,
        ).wait_recv()


def gather_columns(w_out):
    n = lax.axis_size("expert")
    rows, cols = w_out.shape
    return pl.pallas_call(
        lambda *refs: gather_kernel(n, *refs),
        out_shape=jax.ShapeDtypeStruct((rows, cols * n), w_out.dtype),
        in_specs=[pl.BlockSpec(memory_space=pl.ANY)],
        out_specs=pl.BlockSpec(memory_space=pl.ANY),
        scratch_shapes=[
            pltpu.SemaphoreType.DMA((n,)),
            pltpu.SemaphoreType.DMA((n,)),
            pltpu.SemaphoreType.DMA(()),
        ],
        compiler_params=pltpu.CompilerParams(collective_id=0, has_side_effects=True),
    )(w_out)


def project(context, w_out):
    n_x = lax.axis_size("xlo")
    n_c = lax.axis_size("core")
    rows = context.shape[0] // (n_x * n_c)
    context = context.reshape(n_x, n_c, rows, -1).transpose(1, 0, 2, 3).reshape(n_x * n_c * rows, -1)
    partial_sums = jnp.dot(
        context,
        gather_columns(w_out),
        preferred_element_type=jnp.float32,
    )
    width = partial_sums.shape[1]
    chip_sums = lax.psum_scatter(partial_sums, "core", scatter_dimension=0, tiled=True)
    chip_sums = chip_sums.reshape(n_x, rows, width)
    me = lax.axis_index("xlo")
    own = lax.dynamic_index_in_dim(chip_sums, me, axis=0, keepdims=False)
    other = lax.dynamic_index_in_dim(chip_sums, 1 - me, axis=0, keepdims=False)
    arrived = lax.ppermute(other.astype(jnp.bfloat16), "xlo", perm=[(0, 1), (1, 0)])
    return own + arrived.astype(jnp.float32)


def on_device(hidden_in, context, w_out, norm_gain, expert_ids, route_weight, w_gate_up, w_down):
    tok_count, width = hidden_in.shape
    chunks = width // LANES
    projected = project(context, w_out)
    residual = hidden_in.astype(jnp.float32) + projected
    attended = residual.astype(jnp.bfloat16)
    inverse = lax.rsqrt(jnp.mean(residual * residual, axis=1, keepdims=True) + 1e-06)
    normed = (residual * inverse * norm_gain[None, :]).astype(jnp.bfloat16)
    top_count = expert_ids.shape[1]
    experts_all = lax.axis_size(ALL)
    capacity = tok_count * top_count * 9 // (8 * experts_all)
    rows_all = experts_all * capacity
    chosen = expert_ids.reshape(-1)
    onehot = (chosen[:, None] == jnp.arange(experts_all, dtype=jnp.int32)[None, :]).astype(
        jnp.int32
    )
    before = jnp.cumsum(onehot, axis=0) - onehot
    slots = jnp.sum(before * onehot, axis=1)
    target = chosen * capacity + slots
    token_index = jnp.arange(tok_count * top_count, dtype=jnp.int32) // top_count
    source = jnp.full((rows_all,), tok_count, jnp.int32).at[target].set(token_index)
    normed3 = jnp.concatenate(
        [normed.reshape(tok_count, chunks, LANES), jnp.zeros((1, chunks, LANES), jnp.bfloat16)],
        axis=0,
    )
    send = jnp.take(normed3, source, axis=0, mode="clip")
    send = send.reshape(experts_all, capacity * chunks, LANES)
    received = lax.all_to_all(send, ALL, split_axis=0, concat_axis=0, tiled=True)
    outputs = expert_block(received.reshape(rows_all, width), w_gate_up, w_down)
    outputs = outputs.reshape(experts_all, capacity * chunks, LANES)
    returned = lax.all_to_all(outputs, ALL, split_axis=0, concat_axis=0, tiled=True)
    returned = returned.reshape(rows_all, chunks, LANES)
    picked = jnp.take(returned, target, axis=0, mode="clip").reshape(tok_count, top_count, chunks, LANES)
    moe_sum = jnp.sum(route_weight[:, :, None, None] * picked.astype(jnp.float32), axis=1)
    mixed = (residual + moe_sum.reshape(tok_count, width)).astype(jnp.bfloat16)
    return (attended, mixed)


def solution(mesh):
    n_expert = mesh.shape["expert"]
    n_tensor = mesh.shape["tensor"]
    n_core = 2 if n_tensor % 2 == 0 else 1
    devices = np.asarray(mesh.devices).reshape(n_expert, n_tensor // n_core, n_core)
    mesh3 = Mesh(devices, ALL)
    tensor = ("xlo", "core")
    in_specs = (
        P(ALL, None),
        P("expert", tensor),
        P(tensor, "expert"),
        P(),
        P(ALL, None),
        P(ALL, None),
        P(ALL, None, None),
        P(ALL, None, None),
    )
    out_specs = (P(ALL, None), P(ALL, None))
    return jax.shard_map(
        on_device, mesh=mesh3, in_specs=in_specs, out_specs=out_specs, check_vma=False
    )
```

```python
import jax
import jax.numpy as jnp
import numpy as np
from jax import lax
from jax.experimental import pallas as pl
from jax.experimental.pallas import tpu as pltpu
from jax.sharding import Mesh
from jax.sharding import PartitionSpec as P

LANES = 128
EXPERT = ("y", "xhi", "z")
ALL = EXPERT + ("xlo", "core")


def expert_block(received, w_gate_up, w_down):
    hidden_units = w_down.shape[1]
    gate_and_up = jnp.dot(received, w_gate_up[0], preferred_element_type=jnp.float32)
    activated = (jax.nn.silu(gate_and_up[:, :hidden_units]) * gate_and_up[:, hidden_units:]).astype(
        jnp.bfloat16
    )
    return jnp.dot(activated, w_down[0], preferred_element_type=jnp.float32).astype(jnp.bfloat16)


def gather_columns(w_out):
    rows, cols = w_out.shape
    staged = lax.all_gather(w_out, "xhi", axis=0)
    staged = lax.all_gather(staged, "z", axis=0)
    staged = lax.all_gather(staged, "y", axis=0)
    return staged.transpose(3, 0, 2, 1, 4).reshape(rows, -1)


def project(context, w_out):
    n_x = lax.axis_size("xlo")
    n_c = lax.axis_size("core")
    rows = context.shape[0] // (n_x * n_c)
    context = context.reshape(n_x, n_c, rows, -1).transpose(1, 0, 2, 3).reshape(n_x * n_c * rows, -1)
    partial_sums = jnp.dot(
        context,
        gather_columns(w_out),
        preferred_element_type=jnp.float32,
    )
    width = partial_sums.shape[1]
    chip_sums = lax.psum_scatter(partial_sums, "core", scatter_dimension=0, tiled=True)
    chip_sums = chip_sums.reshape(n_x, rows, width)
    me = lax.axis_index("xlo")
    own = lax.dynamic_index_in_dim(chip_sums, me, axis=0, keepdims=False)
    other = lax.dynamic_index_in_dim(chip_sums, 1 - me, axis=0, keepdims=False)
    arrived = lax.ppermute(other.astype(jnp.bfloat16), "xlo", perm=[(0, 1), (1, 0)])
    return own + arrived.astype(jnp.float32)


def on_device(hidden_in, context, w_out, norm_gain, expert_ids, route_weight, w_gate_up, w_down):
    tok_count, width = hidden_in.shape
    chunks = width // LANES
    projected = project(context, w_out)
    residual = hidden_in.astype(jnp.float32) + projected
    attended = residual.astype(jnp.bfloat16)
    inverse = lax.rsqrt(jnp.mean(residual * residual, axis=1, keepdims=True) + 1e-06)
    normed = (residual * inverse * norm_gain[None, :]).astype(jnp.bfloat16)
    top_count = expert_ids.shape[1]
    experts_all = lax.axis_size(ALL)
    capacity = tok_count * top_count * 9 // (8 * experts_all)
    rows_all = experts_all * capacity
    chosen = expert_ids.reshape(-1)
    onehot = (chosen[:, None] == jnp.arange(experts_all, dtype=jnp.int32)[None, :]).astype(
        jnp.int32
    )
    before = jnp.cumsum(onehot, axis=0) - onehot
    slots = jnp.sum(before * onehot, axis=1)
    target = chosen * capacity + slots
    token_index = jnp.arange(tok_count * top_count, dtype=jnp.int32) // top_count
    source = jnp.full((rows_all,), tok_count, jnp.int32).at[target].set(token_index)
    normed3 = jnp.concatenate(
        [normed.reshape(tok_count, chunks, LANES), jnp.zeros((1, chunks, LANES), jnp.bfloat16)],
        axis=0,
    )
    send = jnp.take(normed3, source, axis=0, mode="clip")
    send = send.reshape(experts_all, capacity * chunks, LANES)
    received = lax.all_to_all(send, ALL, split_axis=0, concat_axis=0, tiled=True)
    outputs = expert_block(received.reshape(rows_all, width), w_gate_up, w_down)
    outputs = outputs.reshape(experts_all, capacity * chunks, LANES)
    returned = lax.all_to_all(outputs, ALL, split_axis=0, concat_axis=0, tiled=True)
    returned = returned.reshape(rows_all, chunks, LANES)
    picked = jnp.take(returned, target, axis=0, mode="clip").reshape(tok_count, top_count, chunks, LANES)
    moe_sum = jnp.sum(route_weight[:, :, None, None] * picked.astype(jnp.float32), axis=1)
    mixed = (residual + moe_sum.reshape(tok_count, width)).astype(jnp.bfloat16)
    return (attended, mixed)


def solution(mesh):
    n_expert = mesh.shape["expert"]
    n_tensor = mesh.shape["tensor"]
    n_core = 2 if n_tensor % 2 == 0 else 1
    n_xhi = 2 if n_expert % 32 == 0 else 1
    n_z = 4 if n_expert % 4 == 0 else 1
    shape = (n_expert // (n_xhi * n_z), n_xhi, n_z, n_tensor // n_core, n_core)
    mesh3 = Mesh(np.asarray(mesh.devices).reshape(shape), ALL)
    tensor = ("xlo", "core")
    in_specs = (
        P(ALL, None),
        P(EXPERT, tensor),
        P(tensor, EXPERT),
        P(),
        P(ALL, None),
        P(ALL, None),
        P(ALL, None, None),
        P(ALL, None, None),
    )
    out_specs = (P(ALL, None), P(ALL, None))
    return jax.shard_map(
        on_device, mesh=mesh3, in_specs=in_specs, out_specs=out_specs, check_vma=False
    )
```

```python
import jax
import jax.numpy as jnp
import numpy as np
from jax import lax
from jax.experimental import pallas as pl
from jax.experimental.pallas import tpu as pltpu
from jax.sharding import Mesh
from jax.sharding import PartitionSpec as P

LANES = 128
EXPERT = ("y", "xhi", "z")
ALL = EXPERT + ("xlo", "core")


def expert_block(received, w_gate_up, w_down):
    hidden_units = w_down.shape[1]
    gate_and_up = jnp.dot(received, w_gate_up[0], preferred_element_type=jnp.float32)
    activated = (jax.nn.silu(gate_and_up[:, :hidden_units]) * gate_and_up[:, hidden_units:]).astype(
        jnp.bfloat16
    )
    return jnp.dot(activated, w_down[0], preferred_element_type=jnp.float32).astype(jnp.bfloat16)


def gather_columns(w_out):
    rows, cols = w_out.shape
    staged = lax.all_gather(w_out, "xhi", axis=0)
    staged = lax.all_gather(staged, "z", axis=0)
    staged = lax.all_gather(staged, "y", axis=0)
    return staged.transpose(3, 0, 2, 1, 4).reshape(rows, -1)


def project(context, w_out):
    n_x = lax.axis_size("xlo")
    n_c = lax.axis_size("core")
    rows = context.shape[0] // (n_x * n_c)
    context = context.reshape(n_x, n_c, rows, -1).transpose(1, 0, 2, 3).reshape(n_x * n_c * rows, -1)
    partial_sums = jnp.dot(
        context,
        gather_columns(w_out),
        preferred_element_type=jnp.float32,
    )
    width = partial_sums.shape[1]
    chip_sums = lax.psum_scatter(partial_sums, "core", scatter_dimension=0, tiled=True)
    chip_sums = chip_sums.reshape(n_x, rows, width)
    me = lax.axis_index("xlo")
    own = lax.dynamic_index_in_dim(chip_sums, me, axis=0, keepdims=False)
    other = lax.dynamic_index_in_dim(chip_sums, 1 - me, axis=0, keepdims=False)
    arrived = lax.ppermute(other.astype(jnp.bfloat16), "xlo", perm=[(0, 1), (1, 0)])
    return own + arrived.astype(jnp.float32)


def on_device(hidden_in, context, w_out, norm_gain, expert_ids, route_weight, w_gate_up, w_down):
    tok_count, width = hidden_in.shape
    chunks = width // LANES
    projected = project(context, w_out)
    residual = hidden_in.astype(jnp.float32) + projected
    attended = residual.astype(jnp.bfloat16)
    inverse = lax.rsqrt(jnp.mean(residual * residual, axis=1, keepdims=True) + 1e-06)
    normed = (residual * inverse * norm_gain[None, :]).astype(jnp.bfloat16)
    top_count = expert_ids.shape[1]
    experts_all = lax.axis_size(ALL)
    capacity = tok_count * top_count * 9 // (8 * experts_all)
    rows_all = experts_all * capacity
    chosen = expert_ids.reshape(-1)
    onehot = (chosen[:, None] == jnp.arange(experts_all, dtype=jnp.int32)[None, :]).astype(
        jnp.int32
    )
    before = jnp.cumsum(onehot, axis=0) - onehot
    slots = jnp.sum(before * onehot, axis=1)
    target = chosen * capacity + slots
    token_index = jnp.arange(tok_count * top_count, dtype=jnp.int32) // top_count
    source = jnp.full((rows_all,), tok_count, jnp.int32).at[target].set(token_index)
    normed3 = jnp.concatenate(
        [normed.reshape(tok_count, chunks, LANES), jnp.zeros((1, chunks, LANES), jnp.bfloat16)],
        axis=0,
    )
    send = jnp.take(normed3, source, axis=0, mode="clip")
    send = send.reshape(experts_all, capacity * chunks, LANES)
    first = (capacity + 1) // 2
    returned = []
    for lo, hi in ((0, first), (first, capacity)):
        part = send[:, lo * chunks : hi * chunks]
        received = lax.all_to_all(part, ALL, split_axis=0, concat_axis=0, tiled=True)
        outputs = expert_block(
            received.reshape(experts_all * (hi - lo), width), w_gate_up, w_down
        )
        outputs = outputs.reshape(experts_all, (hi - lo) * chunks, LANES)
        returned.append(lax.all_to_all(outputs, ALL, split_axis=0, concat_axis=0, tiled=True))
    returned = jnp.concatenate(returned, axis=1).reshape(rows_all, chunks, LANES)
    picked = jnp.take(returned, target, axis=0, mode="clip").reshape(tok_count, top_count, chunks, LANES)
    moe_sum = jnp.sum(route_weight[:, :, None, None] * picked.astype(jnp.float32), axis=1)
    mixed = (residual + moe_sum.reshape(tok_count, width)).astype(jnp.bfloat16)
    return (attended, mixed)


def solution(mesh):
    n_expert = mesh.shape["expert"]
    n_tensor = mesh.shape["tensor"]
    n_core = 2 if n_tensor % 2 == 0 else 1
    n_xhi = 2 if n_expert % 32 == 0 else 1
    n_z = 4 if n_expert % 4 == 0 else 1
    shape = (n_expert // (n_xhi * n_z), n_xhi, n_z, n_tensor // n_core, n_core)
    mesh3 = Mesh(np.asarray(mesh.devices).reshape(shape), ALL)
    tensor = ("xlo", "core")
    in_specs = (
        P(ALL, None),
        P(EXPERT, tensor),
        P(tensor, EXPERT),
        P(),
        P(ALL, None),
        P(ALL, None),
        P(ALL, None, None),
        P(ALL, None, None),
    )
    out_specs = (P(ALL, None), P(ALL, None))
    return jax.shard_map(
        on_device, mesh=mesh3, in_specs=in_specs, out_specs=out_specs, check_vma=False
    )
```

```python
import jax
import jax.numpy as jnp
import numpy as np
from jax import lax
from jax.experimental import pallas as pl
from jax.experimental.pallas import tpu as pltpu
from jax.sharding import Mesh
from jax.sharding import PartitionSpec as P

LANES = 128
EXPERT = ("y", "xhi", "z")
ALL = EXPERT + ("xlo", "core")


def expert_block(received, w_gate_up, w_down):
    hidden_units = w_down.shape[1]
    gate_and_up = jnp.dot(received, w_gate_up[0], preferred_element_type=jnp.float32)
    activated = (jax.nn.silu(gate_and_up[:, :hidden_units]) * gate_and_up[:, hidden_units:]).astype(
        jnp.bfloat16
    )
    return jnp.dot(activated, w_down[0], preferred_element_type=jnp.float32).astype(jnp.bfloat16)


def gather_columns(w_out):
    rows, cols = w_out.shape
    staged = lax.all_gather(w_out, "xhi", axis=0)
    staged = lax.all_gather(staged, "z", axis=0)
    staged = lax.all_gather(staged, "y", axis=0)
    return staged.transpose(3, 0, 2, 1, 4).reshape(rows, -1)


def project(context, w_out):
    n_x = lax.axis_size("xlo")
    n_c = lax.axis_size("core")
    rows = context.shape[0] // (n_x * n_c)
    context = context.reshape(n_x, n_c, rows, -1).transpose(1, 0, 2, 3).reshape(n_x * n_c * rows, -1)
    partial_sums = jnp.dot(
        context,
        gather_columns(w_out),
        preferred_element_type=jnp.float32,
    )
    width = partial_sums.shape[1]
    chip_sums = lax.psum_scatter(partial_sums, "core", scatter_dimension=0, tiled=True)
    chip_sums = chip_sums.reshape(n_x, rows, width)
    me = lax.axis_index("xlo")
    own = lax.dynamic_index_in_dim(chip_sums, me, axis=0, keepdims=False)
    other = lax.dynamic_index_in_dim(chip_sums, 1 - me, axis=0, keepdims=False)
    arrived = lax.ppermute(other.astype(jnp.bfloat16), "xlo", perm=[(0, 1), (1, 0)])
    return own + arrived.astype(jnp.float32)


def on_device(hidden_in, context, w_out, norm_gain, expert_ids, route_weight, w_gate_up, w_down):
    tok_count, width = hidden_in.shape
    chunks = width // LANES
    projected = project(context, w_out)
    residual = hidden_in.astype(jnp.float32) + projected
    attended = residual.astype(jnp.bfloat16)
    inverse = lax.rsqrt(jnp.mean(residual * residual, axis=1, keepdims=True) + 1e-06)
    normed = (residual * inverse * norm_gain[None, :]).astype(jnp.bfloat16)
    top_count = expert_ids.shape[1]
    experts_all = lax.axis_size(ALL)
    capacity = tok_count * top_count * 9 // (8 * experts_all)
    rows_all = experts_all * capacity
    chosen = expert_ids.reshape(-1)
    onehot = (chosen[:, None] == jnp.arange(experts_all, dtype=jnp.int32)[None, :]).astype(
        jnp.int32
    )
    before = jnp.cumsum(onehot, axis=0) - onehot
    slots = jnp.sum(before * onehot, axis=1)
    target = chosen * capacity + slots
    token_index = jnp.arange(tok_count * top_count, dtype=jnp.int32) // top_count
    source = jnp.full((rows_all,), tok_count, jnp.int32).at[target].set(token_index)
    source = source.reshape(experts_all, capacity)
    normed3 = jnp.concatenate(
        [normed.reshape(tok_count, chunks, LANES), jnp.zeros((1, chunks, LANES), jnp.bfloat16)],
        axis=0,
    )
    weights = route_weight.reshape(-1)
    groups = 3 if capacity % 3 == 0 else 2
    bounds = [capacity * g // groups for g in range(groups + 1)]
    moe_sum = None
    for lo, hi in zip(bounds[:-1], bounds[1:]):
        size = hi - lo
        send = jnp.take(normed3, source[:, lo:hi].reshape(-1), axis=0, mode="clip")
        send = send.reshape(experts_all, size * chunks, LANES)
        received = lax.all_to_all(send, ALL, split_axis=0, concat_axis=0, tiled=True)
        outputs = expert_block(received.reshape(experts_all * size, width), w_gate_up, w_down)
        outputs = outputs.reshape(experts_all, size * chunks, LANES)
        returned = lax.all_to_all(outputs, ALL, split_axis=0, concat_axis=0, tiled=True)
        returned = returned.reshape(experts_all * size, chunks, LANES)
        inside = (slots >= lo) & (slots < hi)
        picked = jnp.take(returned, chosen * size + slots - lo, axis=0, mode="clip")
        scaled = jnp.where(inside, weights, 0.0)[:, None, None] * picked.astype(jnp.float32)
        part = jnp.sum(scaled.reshape(tok_count, top_count, chunks, LANES), axis=1)
        moe_sum = part if moe_sum is None else moe_sum + part
    mixed = (residual + moe_sum.reshape(tok_count, width)).astype(jnp.bfloat16)
    return (attended, mixed)


def solution(mesh):
    n_expert = mesh.shape["expert"]
    n_tensor = mesh.shape["tensor"]
    n_core = 2 if n_tensor % 2 == 0 else 1
    n_xhi = 2 if n_expert % 32 == 0 else 1
    n_z = 4 if n_expert % 4 == 0 else 1
    shape = (n_expert // (n_xhi * n_z), n_xhi, n_z, n_tensor // n_core, n_core)
    mesh3 = Mesh(np.asarray(mesh.devices).reshape(shape), ALL)
    tensor = ("xlo", "core")
    in_specs = (
        P(ALL, None),
        P(EXPERT, tensor),
        P(tensor, EXPERT),
        P(),
        P(ALL, None),
        P(ALL, None),
        P(ALL, None, None),
        P(ALL, None, None),
    )
    out_specs = (P(ALL, None), P(ALL, None))
    return jax.shard_map(
        on_device, mesh=mesh3, in_specs=in_specs, out_specs=out_specs, check_vma=False
    )
```

```python
import jax
import jax.numpy as jnp
import numpy as np
from jax import lax
from jax.experimental import pallas as pl
from jax.experimental.pallas import tpu as pltpu
from jax.sharding import Mesh
from jax.sharding import PartitionSpec as P

LANES = 128
EXPERT = ("y", "xhi", "z")
ALL = EXPERT + ("xlo", "core")


def expert_block(received, w_gate_up, w_down):
    hidden_units = w_down.shape[1]
    gate_and_up = jnp.dot(received, w_gate_up[0], preferred_element_type=jnp.float32)
    activated = (jax.nn.silu(gate_and_up[:, :hidden_units]) * gate_and_up[:, hidden_units:]).astype(
        jnp.bfloat16
    )
    return jnp.dot(activated, w_down[0], preferred_element_type=jnp.float32).astype(jnp.bfloat16)


def gather_columns(w_out):
    rows, cols = w_out.shape
    staged = lax.all_gather(w_out, "xhi", axis=1, tiled=True)
    staged = lax.all_gather(staged, "z", axis=1, tiled=True)
    return lax.all_gather(staged, "y", axis=1, tiled=True)


def project(context, w_out):
    n_x = lax.axis_size("xlo")
    n_c = lax.axis_size("core")
    rows = context.shape[0] // (n_x * n_c)
    context = context.reshape(n_x, n_c, rows, -1).transpose(1, 0, 2, 3).reshape(n_x * n_c * rows, -1)
    partial_sums = jnp.dot(
        context,
        gather_columns(w_out),
        preferred_element_type=jnp.float32,
    )
    width = partial_sums.shape[1]
    chip_sums = lax.psum_scatter(partial_sums, "core", scatter_dimension=0, tiled=True)
    chip_sums = chip_sums.reshape(n_x, rows, width)
    me = lax.axis_index("xlo")
    own = lax.dynamic_index_in_dim(chip_sums, me, axis=0, keepdims=False)
    other = lax.dynamic_index_in_dim(chip_sums, 1 - me, axis=0, keepdims=False)
    arrived = lax.ppermute(other.astype(jnp.bfloat16), "xlo", perm=[(0, 1), (1, 0)])
    summed = own + arrived.astype(jnp.float32)
    n_y, n_z, n_xhi = (lax.axis_size(name) for name in ("y", "z", "xhi"))
    summed = summed.reshape(rows, n_y, n_z, n_xhi, -1).transpose(0, 1, 3, 2, 4)
    return summed.reshape(rows, width)


def on_device(hidden_in, context, w_out, norm_gain, expert_ids, route_weight, w_gate_up, w_down):
    tok_count, width = hidden_in.shape
    chunks = width // LANES
    projected = project(context, w_out)
    residual = hidden_in.astype(jnp.float32) + projected
    attended = residual.astype(jnp.bfloat16)
    inverse = lax.rsqrt(jnp.mean(residual * residual, axis=1, keepdims=True) + 1e-06)
    normed = (residual * inverse * norm_gain[None, :]).astype(jnp.bfloat16)
    top_count = expert_ids.shape[1]
    experts_all = lax.axis_size(ALL)
    capacity = tok_count * top_count * 9 // (8 * experts_all)
    rows_all = experts_all * capacity
    chosen = expert_ids.reshape(-1)
    onehot = (chosen[:, None] == jnp.arange(experts_all, dtype=jnp.int32)[None, :]).astype(
        jnp.int32
    )
    before = jnp.cumsum(onehot, axis=0) - onehot
    slots = jnp.sum(before * onehot, axis=1)
    target = chosen * capacity + slots
    token_index = jnp.arange(tok_count * top_count, dtype=jnp.int32) // top_count
    source = jnp.full((rows_all,), tok_count, jnp.int32).at[target].set(token_index)
    normed3 = jnp.concatenate(
        [normed.reshape(tok_count, chunks, LANES), jnp.zeros((1, chunks, LANES), jnp.bfloat16)],
        axis=0,
    )
    send = jnp.take(normed3, source, axis=0, mode="clip")
    send = send.reshape(experts_all, capacity * chunks, LANES)
    first = (capacity + 1) // 2
    returned = []
    for lo, hi in ((0, first), (first, capacity)):
        part = send[:, lo * chunks : hi * chunks]
        received = lax.all_to_all(part, ALL, split_axis=0, concat_axis=0, tiled=True)
        outputs = expert_block(
            received.reshape(experts_all * (hi - lo), width), w_gate_up, w_down
        )
        outputs = outputs.reshape(experts_all, (hi - lo) * chunks, LANES)
        returned.append(lax.all_to_all(outputs, ALL, split_axis=0, concat_axis=0, tiled=True))
    returned = jnp.concatenate(returned, axis=1).reshape(rows_all, chunks, LANES)
    picked = jnp.take(returned, target, axis=0, mode="clip").reshape(tok_count, top_count, chunks, LANES)
    moe_sum = jnp.sum(route_weight[:, :, None, None] * picked.astype(jnp.float32), axis=1)
    mixed = (residual + moe_sum.reshape(tok_count, width)).astype(jnp.bfloat16)
    return (attended, mixed)


def solution(mesh):
    n_expert = mesh.shape["expert"]
    n_tensor = mesh.shape["tensor"]
    n_core = 2 if n_tensor % 2 == 0 else 1
    n_xhi = 2 if n_expert % 32 == 0 else 1
    n_z = 4 if n_expert % 4 == 0 else 1
    shape = (n_expert // (n_xhi * n_z), n_xhi, n_z, n_tensor // n_core, n_core)
    mesh3 = Mesh(np.asarray(mesh.devices).reshape(shape), ALL)
    tensor = ("xlo", "core")
    in_specs = (
        P(ALL, None),
        P(EXPERT, tensor),
        P(tensor, EXPERT),
        P(),
        P(ALL, None),
        P(ALL, None),
        P(ALL, None, None),
        P(ALL, None, None),
    )
    out_specs = (P(ALL, None), P(ALL, None))
    return jax.shard_map(
        on_device, mesh=mesh3, in_specs=in_specs, out_specs=out_specs, check_vma=False
    )
```

```python
import jax
import jax.numpy as jnp
import numpy as np
from jax import lax
from jax.experimental import pallas as pl
from jax.experimental.pallas import tpu as pltpu
from jax.sharding import Mesh
from jax.sharding import PartitionSpec as P

LANES = 128
EXPERT = ("y", "xhi", "z")
ALL = EXPERT + ("xlo", "core")


def expert_block(received, w_gate_up, w_down):
    hidden_units = w_down.shape[1]
    gate_and_up = jnp.dot(received, w_gate_up[0], preferred_element_type=jnp.float32)
    activated = (jax.nn.silu(gate_and_up[:, :hidden_units]) * gate_and_up[:, hidden_units:]).astype(
        jnp.bfloat16
    )
    return jnp.dot(activated, w_down[0], preferred_element_type=jnp.float32).astype(jnp.bfloat16)


def ring_gather(block, axis):
    n = lax.axis_size(axis)
    me = lax.axis_index(axis)
    plus = [(i, (i + 1) % n) for i in range(n)]
    minus = [(i, (i - 1) % n) for i in range(n)]
    from_left = lax.ppermute(block, axis, perm=plus)
    from_right = lax.ppermute(block, axis, perm=minus)
    half = block.shape[-1] // 2
    far = jnp.concatenate(
        [
            lax.ppermute(from_left[..., :half], axis, perm=plus),
            lax.ppermute(from_right[..., half:], axis, perm=minus),
        ],
        axis=-1,
    )
    by_step = jnp.stack([block, from_right, far, from_left])
    order = (jnp.arange(n, dtype=jnp.int32) - me) % n
    return jnp.take(by_step, order, axis=0)


def gather_columns(w_out):
    staged = lax.all_gather(w_out, "xhi", axis=0)
    first = lax.all_gather(staged[0], "z", axis=1, tiled=True)
    first = lax.all_gather(first, "y", axis=1, tiled=True)
    if staged.shape[0] == 1:
        return first, None
    second = ring_gather(staged[1], "y")
    second = ring_gather(second, "z")
    return first, second


def project(context, w_out):
    n_x = lax.axis_size("xlo")
    n_c = lax.axis_size("core")
    rows = context.shape[0] // (n_x * n_c)
    context = context.reshape(n_x, n_c, rows, -1).transpose(1, 0, 2, 3).reshape(n_x * n_c * rows, -1)
    first, second = gather_columns(w_out)
    partial_sums = jnp.dot(context, first, preferred_element_type=jnp.float32)
    if second is not None:
        other = jnp.einsum("th,zyhl->tyzl", context, second, preferred_element_type=jnp.float32)
        partial_sums = jnp.concatenate(
            [partial_sums, other.reshape(other.shape[0], -1)], axis=1
        )
    width = partial_sums.shape[1]
    chip_sums = lax.psum_scatter(partial_sums, "core", scatter_dimension=0, tiled=True)
    chip_sums = chip_sums.reshape(n_x, rows, width)
    me = lax.axis_index("xlo")
    own = lax.dynamic_index_in_dim(chip_sums, me, axis=0, keepdims=False)
    other = lax.dynamic_index_in_dim(chip_sums, 1 - me, axis=0, keepdims=False)
    arrived = lax.ppermute(other.astype(jnp.bfloat16), "xlo", perm=[(0, 1), (1, 0)])
    summed = own + arrived.astype(jnp.float32)
    n_y, n_xhi = lax.axis_size("y"), lax.axis_size("xhi")
    summed = summed.reshape(rows, n_xhi, n_y, -1).transpose(0, 2, 1, 3)
    return summed.reshape(rows, width)


def on_device(hidden_in, context, w_out, norm_gain, expert_ids, route_weight, w_gate_up, w_down):
    tok_count, width = hidden_in.shape
    chunks = width // LANES
    projected = project(context, w_out)
    residual = hidden_in.astype(jnp.float32) + projected
    attended = residual.astype(jnp.bfloat16)
    inverse = lax.rsqrt(jnp.mean(residual * residual, axis=1, keepdims=True) + 1e-06)
    normed = (residual * inverse * norm_gain[None, :]).astype(jnp.bfloat16)
    top_count = expert_ids.shape[1]
    experts_all = lax.axis_size(ALL)
    capacity = tok_count * top_count * 9 // (8 * experts_all)
    rows_all = experts_all * capacity
    chosen = expert_ids.reshape(-1)
    onehot = (chosen[:, None] == jnp.arange(experts_all, dtype=jnp.int32)[None, :]).astype(
        jnp.int32
    )
    before = jnp.cumsum(onehot, axis=0) - onehot
    slots = jnp.sum(before * onehot, axis=1)
    target = chosen * capacity + slots
    token_index = jnp.arange(tok_count * top_count, dtype=jnp.int32) // top_count
    source = jnp.full((rows_all,), tok_count, jnp.int32).at[target].set(token_index)
    normed3 = jnp.concatenate(
        [normed.reshape(tok_count, chunks, LANES), jnp.zeros((1, chunks, LANES), jnp.bfloat16)],
        axis=0,
    )
    send = jnp.take(normed3, source, axis=0, mode="clip")
    send = send.reshape(experts_all, capacity * chunks, LANES)
    first = (capacity + 1) // 2
    returned = []
    for lo, hi in ((0, first), (first, capacity)):
        part = send[:, lo * chunks : hi * chunks]
        received = lax.all_to_all(part, ALL, split_axis=0, concat_axis=0, tiled=True)
        outputs = expert_block(
            received.reshape(experts_all * (hi - lo), width), w_gate_up, w_down
        )
        outputs = outputs.reshape(experts_all, (hi - lo) * chunks, LANES)
        returned.append(lax.all_to_all(outputs, ALL, split_axis=0, concat_axis=0, tiled=True))
    returned = jnp.concatenate(returned, axis=1).reshape(rows_all, chunks, LANES)
    picked = jnp.take(returned, target, axis=0, mode="clip").reshape(tok_count, top_count, chunks, LANES)
    moe_sum = jnp.sum(route_weight[:, :, None, None] * picked.astype(jnp.float32), axis=1)
    mixed = (residual + moe_sum.reshape(tok_count, width)).astype(jnp.bfloat16)
    return (attended, mixed)


def solution(mesh):
    n_expert = mesh.shape["expert"]
    n_tensor = mesh.shape["tensor"]
    n_core = 2 if n_tensor % 2 == 0 else 1
    n_xhi = 2 if n_expert % 32 == 0 else 1
    n_z = 4 if n_expert % 4 == 0 else 1
    shape = (n_expert // (n_xhi * n_z), n_xhi, n_z, n_tensor // n_core, n_core)
    mesh3 = Mesh(np.asarray(mesh.devices).reshape(shape), ALL)
    tensor = ("xlo", "core")
    in_specs = (
        P(ALL, None),
        P(EXPERT, tensor),
        P(tensor, EXPERT),
        P(),
        P(ALL, None),
        P(ALL, None),
        P(ALL, None, None),
        P(ALL, None, None),
    )
    out_specs = (P(ALL, None), P(ALL, None))
    return jax.shard_map(
        on_device, mesh=mesh3, in_specs=in_specs, out_specs=out_specs, check_vma=False
    )
```

```python
import jax
import jax.numpy as jnp
import numpy as np
from jax import lax
from jax.experimental import pallas as pl
from jax.experimental.pallas import tpu as pltpu
from jax.sharding import Mesh
from jax.sharding import PartitionSpec as P

LANES = 128
EXPERT = ("y", "xhi", "z")
ALL = EXPERT + ("xlo", "core")


def expert_block(received, w_gate_up, w_down):
    hidden_units = w_down.shape[1]
    gate_and_up = jnp.dot(received, w_gate_up[0], preferred_element_type=jnp.float32)
    activated = (jax.nn.silu(gate_and_up[:, :hidden_units]) * gate_and_up[:, hidden_units:]).astype(
        jnp.bfloat16
    )
    return jnp.dot(activated, w_down[0], preferred_element_type=jnp.float32).astype(jnp.bfloat16)


def ring_gather(block, axis):
    n = lax.axis_size(axis)
    plus = [(i, (i + 1) % n) for i in range(n)]
    minus = [(i, (i - 1) % n) for i in range(n)]
    from_left = lax.ppermute(block, axis, perm=plus)
    from_right = lax.ppermute(block, axis, perm=minus)
    half = block.shape[-1] // 2
    far_first = lax.ppermute(from_left[:, :half], axis, perm=plus)
    far_second = lax.ppermute(from_right[:, half:], axis, perm=minus)
    return [block, from_right, far_first, far_second, from_left]


def gather_columns(w_out):
    staged = lax.all_gather(w_out, "xhi", axis=0)
    first = lax.all_gather(staged[0], "z", axis=1, tiled=True)
    first = lax.all_gather(first, "y", axis=1, tiled=True)
    second = jnp.concatenate(ring_gather(staged[1], "y"), axis=1)
    return jnp.concatenate([first] + ring_gather(second, "z"), axis=1)


def project(context, w_out):
    n_x = lax.axis_size("xlo")
    n_c = lax.axis_size("core")
    rows = context.shape[0] // (n_x * n_c)
    context = context.reshape(n_x, n_c, rows, -1).transpose(1, 0, 2, 3).reshape(n_x * n_c * rows, -1)
    partial_sums = jnp.dot(context, gather_columns(w_out), preferred_element_type=jnp.float32)
    width = partial_sums.shape[1]
    chip_sums = lax.psum_scatter(partial_sums, "core", scatter_dimension=0, tiled=True)
    chip_sums = chip_sums.reshape(n_x, rows, width)
    me = lax.axis_index("xlo")
    own = lax.dynamic_index_in_dim(chip_sums, me, axis=0, keepdims=False)
    other = lax.dynamic_index_in_dim(chip_sums, 1 - me, axis=0, keepdims=False)
    arrived = lax.ppermute(other.astype(jnp.bfloat16), "xlo", perm=[(0, 1), (1, 0)])
    summed = own + arrived.astype(jnp.float32)
    n_y, n_z = lax.axis_size("y"), lax.axis_size("z")
    summed = summed.reshape(rows, 2, n_y * n_z, -1)
    by_rings = summed[:, 1].reshape(rows, n_z, n_y, -1)
    z_order = (jnp.arange(n_z, dtype=jnp.int32) - lax.axis_index("z")) % n_z
    y_order = (jnp.arange(n_y, dtype=jnp.int32) - lax.axis_index("y")) % n_y
    by_rings = jnp.take(jnp.take(by_rings, z_order, axis=1), y_order, axis=2)
    by_rings = by_rings.transpose(0, 2, 1, 3).reshape(rows, n_y * n_z, -1)
    summed = jnp.stack([summed[:, 0], by_rings], axis=1).reshape(rows, 2, n_y, n_z, -1)
    return summed.transpose(0, 2, 1, 3, 4).reshape(rows, width)


def on_device(hidden_in, context, w_out, norm_gain, expert_ids, route_weight, w_gate_up, w_down):
    tok_count, width = hidden_in.shape
    chunks = width // LANES
    projected = project(context, w_out)
    residual = hidden_in.astype(jnp.float32) + projected
    attended = residual.astype(jnp.bfloat16)
    inverse = lax.rsqrt(jnp.mean(residual * residual, axis=1, keepdims=True) + 1e-06)
    normed = (residual * inverse * norm_gain[None, :]).astype(jnp.bfloat16)
    top_count = expert_ids.shape[1]
    experts_all = lax.axis_size(ALL)
    capacity = tok_count * top_count * 9 // (8 * experts_all)
    rows_all = experts_all * capacity
    chosen = expert_ids.reshape(-1)
    onehot = (chosen[:, None] == jnp.arange(experts_all, dtype=jnp.int32)[None, :]).astype(
        jnp.int32
    )
    before = jnp.cumsum(onehot, axis=0) - onehot
    slots = jnp.sum(before * onehot, axis=1)
    target = chosen * capacity + slots
    token_index = jnp.arange(tok_count * top_count, dtype=jnp.int32) // top_count
    source = jnp.full((rows_all,), tok_count, jnp.int32).at[target].set(token_index)
    normed3 = jnp.concatenate(
        [normed.reshape(tok_count, chunks, LANES), jnp.zeros((1, chunks, LANES), jnp.bfloat16)],
        axis=0,
    )
    send = jnp.take(normed3, source, axis=0, mode="clip")
    send = send.reshape(experts_all, capacity * chunks, LANES)
    first = (capacity + 1) // 2
    returned = []
    for lo, hi in ((0, first), (first, capacity)):
        part = send[:, lo * chunks : hi * chunks]
        received = lax.all_to_all(part, ALL, split_axis=0, concat_axis=0, tiled=True)
        outputs = expert_block(
            received.reshape(experts_all * (hi - lo), width), w_gate_up, w_down
        )
        outputs = outputs.reshape(experts_all, (hi - lo) * chunks, LANES)
        returned.append(lax.all_to_all(outputs, ALL, split_axis=0, concat_axis=0, tiled=True))
    returned = jnp.concatenate(returned, axis=1).reshape(rows_all, chunks, LANES)
    picked = jnp.take(returned, target, axis=0, mode="clip").reshape(tok_count, top_count, chunks, LANES)
    moe_sum = jnp.sum(route_weight[:, :, None, None] * picked.astype(jnp.float32), axis=1)
    mixed = (residual + moe_sum.reshape(tok_count, width)).astype(jnp.bfloat16)
    return (attended, mixed)


def solution(mesh):
    n_expert = mesh.shape["expert"]
    n_tensor = mesh.shape["tensor"]
    n_core = 2 if n_tensor % 2 == 0 else 1
    n_xhi = 2 if n_expert % 32 == 0 else 1
    n_z = 4 if n_expert % 4 == 0 else 1
    shape = (n_expert // (n_xhi * n_z), n_xhi, n_z, n_tensor // n_core, n_core)
    mesh3 = Mesh(np.asarray(mesh.devices).reshape(shape), ALL)
    tensor = ("xlo", "core")
    in_specs = (
        P(ALL, None),
        P(EXPERT, tensor),
        P(tensor, EXPERT),
        P(),
        P(ALL, None),
        P(ALL, None),
        P(ALL, None, None),
        P(ALL, None, None),
    )
    out_specs = (P(ALL, None), P(ALL, None))
    return jax.shard_map(
        on_device, mesh=mesh3, in_specs=in_specs, out_specs=out_specs, check_vma=False
    )
```

```python
import jax
import jax.numpy as jnp
import numpy as np
from jax import lax
from jax.experimental import pallas as pl
from jax.experimental.pallas import tpu as pltpu
from jax.sharding import Mesh
from jax.sharding import PartitionSpec as P

LANES = 128
EXPERT = ("y", "xhi", "z")
ALL = EXPERT + ("xlo", "core")


def expert_block(received, w_gate_up, w_down):
    hidden_units = w_down.shape[1]
    gate_and_up = jnp.dot(received, w_gate_up[0], preferred_element_type=jnp.float32)
    activated = (jax.nn.silu(gate_and_up[:, :hidden_units]) * gate_and_up[:, hidden_units:]).astype(
        jnp.bfloat16
    )
    return jnp.dot(activated, w_down[0], preferred_element_type=jnp.float32).astype(jnp.bfloat16)


def ring_gather(block, axis):
    n = lax.axis_size(axis)
    me = lax.axis_index(axis)
    plus = [(i, (i + 1) % n) for i in range(n)]
    minus = [(i, (i - 1) % n) for i in range(n)]
    from_left = lax.ppermute(block, axis, perm=plus)
    from_right = lax.ppermute(block, axis, perm=minus)
    half = block.shape[-1] // 2
    far = jnp.concatenate(
        [
            lax.ppermute(from_left[..., :half], axis, perm=plus),
            lax.ppermute(from_right[..., half:], axis, perm=minus),
        ],
        axis=-1,
    )
    by_step = jnp.stack([block, from_right, far, from_left])
    order = (jnp.arange(n, dtype=jnp.int32) - me) % n
    return jnp.take(by_step, order, axis=0)


def gather_columns(w_out):
    staged = lax.all_gather(w_out, "xhi", axis=0)
    first = lax.all_gather(staged[0], "z", axis=1, tiled=True)
    first = lax.all_gather(first, "y", axis=1, tiled=True)
    if staged.shape[0] == 1:
        return first, None
    second = ring_gather(staged[1], "y")
    second = ring_gather(second, "z")
    return first, second


def project(context, w_out):
    n_x = lax.axis_size("xlo")
    n_c = lax.axis_size("core")
    rows = context.shape[0] // (n_x * n_c)
    context = context.reshape(n_x, n_c, rows, -1).transpose(1, 0, 2, 3).reshape(n_x * n_c * rows, -1)
    first, second = gather_columns(w_out)
    partial_sums = jnp.dot(context, first, preferred_element_type=jnp.float32)
    if second is not None:
        other = jnp.einsum("th,zyhl->tyzl", context, second, preferred_element_type=jnp.float32)
        partial_sums = jnp.concatenate(
            [partial_sums, other.reshape(other.shape[0], -1)], axis=1
        )
    width = partial_sums.shape[1]
    chip_sums = lax.psum_scatter(partial_sums, "core", scatter_dimension=0, tiled=True)
    chip_sums = chip_sums.reshape(n_x, rows, width)
    me = lax.axis_index("xlo")
    own = lax.dynamic_index_in_dim(chip_sums, me, axis=0, keepdims=False)
    other = lax.dynamic_index_in_dim(chip_sums, 1 - me, axis=0, keepdims=False)
    arrived = lax.ppermute(other.astype(jnp.bfloat16), "xlo", perm=[(0, 1), (1, 0)])
    summed = own + arrived.astype(jnp.float32)
    n_y, n_xhi = lax.axis_size("y"), lax.axis_size("xhi")
    summed = summed.reshape(rows, n_xhi, n_y, -1).transpose(0, 2, 1, 3)
    return summed.reshape(rows, width)


def on_device(hidden_in, context, w_out, norm_gain, expert_ids, route_weight, w_gate_up, w_down):
    tok_count, width = hidden_in.shape
    chunks = width // LANES
    projected = project(context, w_out)
    residual = hidden_in.astype(jnp.float32) + projected
    attended = residual.astype(jnp.bfloat16)
    inverse = lax.rsqrt(jnp.mean(residual * residual, axis=1, keepdims=True) + 1e-06)
    normed = (residual * inverse * norm_gain[None, :]).astype(jnp.bfloat16)
    top_count = expert_ids.shape[1]
    experts_all = lax.axis_size(ALL)
    capacity = tok_count * top_count * 9 // (8 * experts_all)
    rows_all = experts_all * capacity
    chosen = expert_ids.reshape(-1)
    onehot = (chosen[:, None] == jnp.arange(experts_all, dtype=jnp.int32)[None, :]).astype(
        jnp.int32
    )
    before = jnp.cumsum(onehot, axis=0) - onehot
    slots = jnp.sum(before * onehot, axis=1)
    target = chosen * capacity + slots
    token_index = jnp.arange(tok_count * top_count, dtype=jnp.int32) // top_count
    source = jnp.full((rows_all,), tok_count, jnp.int32).at[target].set(token_index)
    source = source.reshape(experts_all, capacity)
    normed3 = jnp.concatenate(
        [normed.reshape(tok_count, chunks, LANES), jnp.zeros((1, chunks, LANES), jnp.bfloat16)],
        axis=0,
    )
    weights = route_weight.reshape(-1)
    groups = 2
    bounds = [capacity * g // groups for g in range(groups + 1)]
    moe_sum = None
    for lo, hi in zip(bounds[:-1], bounds[1:]):
        size = hi - lo
        send = jnp.take(normed3, source[:, lo:hi].reshape(-1), axis=0, mode="clip")
        send = send.reshape(experts_all, size * chunks, LANES)
        received = lax.all_to_all(send, ALL, split_axis=0, concat_axis=0, tiled=True)
        outputs = expert_block(received.reshape(experts_all * size, width), w_gate_up, w_down)
        outputs = outputs.reshape(experts_all, size * chunks, LANES)
        returned = lax.all_to_all(outputs, ALL, split_axis=0, concat_axis=0, tiled=True)
        returned = returned.reshape(experts_all * size, chunks, LANES)
        inside = (slots >= lo) & (slots < hi)
        picked = jnp.take(returned, chosen * size + slots - lo, axis=0, mode="clip")
        scaled = jnp.where(inside, weights, 0.0)[:, None, None] * picked.astype(jnp.float32)
        part = jnp.sum(scaled.reshape(tok_count, top_count, chunks, LANES), axis=1)
        moe_sum = part if moe_sum is None else moe_sum + part
    mixed = (residual + moe_sum.reshape(tok_count, width)).astype(jnp.bfloat16)
    return (attended, mixed)


def solution(mesh):
    n_expert = mesh.shape["expert"]
    n_tensor = mesh.shape["tensor"]
    n_core = 2 if n_tensor % 2 == 0 else 1
    n_xhi = 2 if n_expert % 32 == 0 else 1
    n_z = 4 if n_expert % 4 == 0 else 1
    shape = (n_expert // (n_xhi * n_z), n_xhi, n_z, n_tensor // n_core, n_core)
    mesh3 = Mesh(np.asarray(mesh.devices).reshape(shape), ALL)
    tensor = ("xlo", "core")
    in_specs = (
        P(ALL, None),
        P(EXPERT, tensor),
        P(tensor, EXPERT),
        P(),
        P(ALL, None),
        P(ALL, None),
        P(ALL, None, None),
        P(ALL, None, None),
    )
    out_specs = (P(ALL, None), P(ALL, None))
    return jax.shard_map(
        on_device, mesh=mesh3, in_specs=in_specs, out_specs=out_specs, check_vma=False
    )
```

```python
import jax
import jax.numpy as jnp
import numpy as np
from jax import lax
from jax.experimental import pallas as pl
from jax.experimental.pallas import tpu as pltpu
from jax.sharding import Mesh
from jax.sharding import PartitionSpec as P

LANES = 128
EXPERT = ("y", "xhi", "z")
ALL = EXPERT + ("xlo", "core")


def expert_block(received, w_gate_up, w_down):
    hidden_units = w_down.shape[1]
    gate_and_up = jnp.dot(received, w_gate_up[0], preferred_element_type=jnp.float32)
    activated = (jax.nn.silu(gate_and_up[:, :hidden_units]) * gate_and_up[:, hidden_units:]).astype(
        jnp.bfloat16
    )
    return jnp.dot(activated, w_down[0], preferred_element_type=jnp.float32).astype(jnp.bfloat16)


def ring_gather(block, axis):
    n = lax.axis_size(axis)
    me = lax.axis_index(axis)
    plus = [(i, (i + 1) % n) for i in range(n)]
    minus = [(i, (i - 1) % n) for i in range(n)]
    from_left = lax.ppermute(block, axis, perm=plus)
    from_right = lax.ppermute(block, axis, perm=minus)
    half = block.shape[-1] // 2
    far = jnp.concatenate(
        [
            lax.ppermute(from_left[..., :half], axis, perm=plus),
            lax.ppermute(from_right[..., half:], axis, perm=minus),
        ],
        axis=-1,
    )
    by_step = jnp.stack([block, from_right, far, from_left])
    order = (jnp.arange(n, dtype=jnp.int32) - me) % n
    return jnp.take(by_step, order, axis=0)


def gather_columns(w_out):
    staged = lax.all_gather(w_out, "xhi", axis=0)
    first = lax.all_gather(staged[0], "y", axis=1, tiled=True)
    first = lax.all_gather(first, "z", axis=1, tiled=True)
    second = ring_gather(staged[1], "z")
    second = ring_gather(second, "y")
    return first, second


def project(context, w_out):
    n_x = lax.axis_size("xlo")
    n_c = lax.axis_size("core")
    rows = context.shape[0] // (n_x * n_c)
    context = context.reshape(n_x, n_c, rows, -1).transpose(1, 0, 2, 3).reshape(n_x * n_c * rows, -1)
    first, second = gather_columns(w_out)
    partial_sums = jnp.dot(context, first, preferred_element_type=jnp.float32)
    other = jnp.einsum("th,yzhl->tyzl", context, second, preferred_element_type=jnp.float32)
    partial_sums = jnp.concatenate([partial_sums, other.reshape(other.shape[0], -1)], axis=1)
    width = partial_sums.shape[1]
    chip_sums = lax.psum_scatter(partial_sums, "core", scatter_dimension=0, tiled=True)
    chip_sums = chip_sums.reshape(n_x, rows, width)
    me = lax.axis_index("xlo")
    own = lax.dynamic_index_in_dim(chip_sums, me, axis=0, keepdims=False)
    other = lax.dynamic_index_in_dim(chip_sums, 1 - me, axis=0, keepdims=False)
    arrived = lax.ppermute(other.astype(jnp.bfloat16), "xlo", perm=[(0, 1), (1, 0)])
    summed = own + arrived.astype(jnp.float32)
    n_y, n_z = lax.axis_size("y"), lax.axis_size("z")
    first = summed[:, : width // 2].reshape(rows, n_z, n_y, -1).transpose(0, 2, 1, 3)
    second = summed[:, width // 2 :].reshape(rows, n_y, n_z, -1)
    return jnp.stack([first, second], axis=2).reshape(rows, width)


def on_device(hidden_in, context, w_out, norm_gain, expert_ids, route_weight, w_gate_up, w_down):
    tok_count, width = hidden_in.shape
    chunks = width // LANES
    projected = project(context, w_out)
    residual = hidden_in.astype(jnp.float32) + projected
    attended = residual.astype(jnp.bfloat16)
    inverse = lax.rsqrt(jnp.mean(residual * residual, axis=1, keepdims=True) + 1e-06)
    normed = (residual * inverse * norm_gain[None, :]).astype(jnp.bfloat16)
    top_count = expert_ids.shape[1]
    experts_all = lax.axis_size(ALL)
    capacity = tok_count * top_count * 9 // (8 * experts_all)
    rows_all = experts_all * capacity
    chosen = expert_ids.reshape(-1)
    onehot = (chosen[:, None] == jnp.arange(experts_all, dtype=jnp.int32)[None, :]).astype(
        jnp.int32
    )
    before = jnp.cumsum(onehot, axis=0) - onehot
    slots = jnp.sum(before * onehot, axis=1)
    target = chosen * capacity + slots
    token_index = jnp.arange(tok_count * top_count, dtype=jnp.int32) // top_count
    source = jnp.full((rows_all,), tok_count, jnp.int32).at[target].set(token_index)
    source = source.reshape(experts_all, capacity)
    normed3 = jnp.concatenate(
        [normed.reshape(tok_count, chunks, LANES), jnp.zeros((1, chunks, LANES), jnp.bfloat16)],
        axis=0,
    )
    weights = route_weight.reshape(-1)
    groups = 2
    bounds = [capacity * g // groups for g in range(groups + 1)]
    moe_sum = None
    for lo, hi in zip(bounds[:-1], bounds[1:]):
        size = hi - lo
        send = jnp.take(normed3, source[:, lo:hi].reshape(-1), axis=0, mode="clip")
        send = send.reshape(experts_all, size * chunks, LANES)
        received = lax.all_to_all(send, ALL, split_axis=0, concat_axis=0, tiled=True)
        outputs = expert_block(received.reshape(experts_all * size, width), w_gate_up, w_down)
        outputs = outputs.reshape(experts_all, size * chunks, LANES)
        returned = lax.all_to_all(outputs, ALL, split_axis=0, concat_axis=0, tiled=True)
        returned = returned.reshape(experts_all * size, chunks, LANES)
        inside = (slots >= lo) & (slots < hi)
        picked = jnp.take(returned, chosen * size + slots - lo, axis=0, mode="clip")
        scaled = jnp.where(inside, weights, 0.0)[:, None, None] * picked.astype(jnp.float32)
        part = jnp.sum(scaled.reshape(tok_count, top_count, chunks, LANES), axis=1)
        moe_sum = part if moe_sum is None else moe_sum + part
    mixed = (residual + moe_sum.reshape(tok_count, width)).astype(jnp.bfloat16)
    return (attended, mixed)


def solution(mesh):
    n_expert = mesh.shape["expert"]
    n_tensor = mesh.shape["tensor"]
    n_core = 2 if n_tensor % 2 == 0 else 1
    n_xhi = 2 if n_expert % 32 == 0 else 1
    n_z = 4 if n_expert % 4 == 0 else 1
    shape = (n_expert // (n_xhi * n_z), n_xhi, n_z, n_tensor // n_core, n_core)
    mesh3 = Mesh(np.asarray(mesh.devices).reshape(shape), ALL)
    tensor = ("xlo", "core")
    in_specs = (
        P(ALL, None),
        P(EXPERT, tensor),
        P(tensor, EXPERT),
        P(),
        P(ALL, None),
        P(ALL, None),
        P(ALL, None, None),
        P(ALL, None, None),
    )
    out_specs = (P(ALL, None), P(ALL, None))
    return jax.shard_map(
        on_device, mesh=mesh3, in_specs=in_specs, out_specs=out_specs, check_vma=False
    )
```

```python
import jax
import jax.numpy as jnp
import numpy as np
from jax import lax
from jax.experimental import pallas as pl
from jax.experimental.pallas import tpu as pltpu
from jax.sharding import Mesh
from jax.sharding import PartitionSpec as P

LANES = 128
EXPERT = ("y", "xhi", "z")
ALL = EXPERT + ("xlo", "core")


def expert_block(received, w_gate_up, w_down):
    hidden_units = w_down.shape[1]
    gate_and_up = jnp.dot(received, w_gate_up[0], preferred_element_type=jnp.float32)
    activated = (jax.nn.silu(gate_and_up[:, :hidden_units]) * gate_and_up[:, hidden_units:]).astype(
        jnp.bfloat16
    )
    return jnp.dot(activated, w_down[0], preferred_element_type=jnp.float32).astype(jnp.bfloat16)


def ring_gather(block, axis):
    n = lax.axis_size(axis)
    me = lax.axis_index(axis)
    plus = [(i, (i + 1) % n) for i in range(n)]
    minus = [(i, (i - 1) % n) for i in range(n)]
    from_left = lax.ppermute(block, axis, perm=plus)
    from_right = lax.ppermute(block, axis, perm=minus)
    half = block.shape[-1] // 2
    far = jnp.concatenate(
        [
            lax.ppermute(from_left[..., :half], axis, perm=plus),
            lax.ppermute(from_right[..., half:], axis, perm=minus),
        ],
        axis=-1,
    )
    by_step = jnp.stack([block, from_right, far, from_left])
    order = (jnp.arange(n, dtype=jnp.int32) - me) % n
    return jnp.take(by_step, order, axis=0)


def gather_columns(w_out):
    staged = lax.all_gather(w_out, "xhi", axis=0)
    first = lax.all_gather(staged[0], "y", axis=1, tiled=True)
    first = lax.all_gather(first, "z", axis=1, tiled=True)
    second = ring_gather(staged[1], "z")
    second = ring_gather(second, "y")
    return first, second


def project(context, w_out):
    n_x = lax.axis_size("xlo")
    n_c = lax.axis_size("core")
    rows = context.shape[0] // (n_x * n_c)
    context = context.reshape(n_x, n_c, rows, -1).transpose(1, 0, 2, 3).reshape(n_x * n_c * rows, -1)
    first, second = gather_columns(w_out)
    partial_sums = jnp.dot(context, first, preferred_element_type=jnp.float32)
    second = second.transpose(2, 0, 1, 3).reshape(second.shape[2], -1)
    other = jnp.dot(context, second, preferred_element_type=jnp.float32)
    partial_sums = jnp.concatenate([partial_sums, other], axis=1)
    width = partial_sums.shape[1]
    chip_sums = lax.psum_scatter(partial_sums, "core", scatter_dimension=0, tiled=True)
    chip_sums = chip_sums.reshape(n_x, rows, width)
    me = lax.axis_index("xlo")
    own = lax.dynamic_index_in_dim(chip_sums, me, axis=0, keepdims=False)
    other = lax.dynamic_index_in_dim(chip_sums, 1 - me, axis=0, keepdims=False)
    arrived = lax.ppermute(other.astype(jnp.bfloat16), "xlo", perm=[(0, 1), (1, 0)])
    summed = own + arrived.astype(jnp.float32)
    n_y, n_z = lax.axis_size("y"), lax.axis_size("z")
    first = summed[:, : width // 2].reshape(rows, n_z, n_y, -1).transpose(0, 2, 1, 3)
    second = summed[:, width // 2 :].reshape(rows, n_y, n_z, -1)
    return jnp.stack([first, second], axis=2).reshape(rows, width)


def on_device(hidden_in, context, w_out, norm_gain, expert_ids, route_weight, w_gate_up, w_down):
    tok_count, width = hidden_in.shape
    chunks = width // LANES
    projected = project(context, w_out)
    residual = hidden_in.astype(jnp.float32) + projected
    attended = residual.astype(jnp.bfloat16)
    inverse = lax.rsqrt(jnp.mean(residual * residual, axis=1, keepdims=True) + 1e-06)
    normed = (residual * inverse * norm_gain[None, :]).astype(jnp.bfloat16)
    top_count = expert_ids.shape[1]
    experts_all = lax.axis_size(ALL)
    capacity = tok_count * top_count * 9 // (8 * experts_all)
    rows_all = experts_all * capacity
    chosen = expert_ids.reshape(-1)
    onehot = (chosen[:, None] == jnp.arange(experts_all, dtype=jnp.int32)[None, :]).astype(
        jnp.int32
    )
    before = jnp.cumsum(onehot, axis=0) - onehot
    slots = jnp.sum(before * onehot, axis=1)
    target = chosen * capacity + slots
    token_index = jnp.arange(tok_count * top_count, dtype=jnp.int32) // top_count
    source = jnp.full((rows_all,), tok_count, jnp.int32).at[target].set(token_index)
    source = source.reshape(experts_all, capacity)
    normed3 = jnp.concatenate(
        [normed.reshape(tok_count, chunks, LANES), jnp.zeros((1, chunks, LANES), jnp.bfloat16)],
        axis=0,
    )
    weights = route_weight.reshape(-1)
    groups = 2
    bounds = [capacity * g // groups for g in range(groups + 1)]
    moe_sum = None
    for lo, hi in zip(bounds[:-1], bounds[1:]):
        size = hi - lo
        send = jnp.take(normed3, source[:, lo:hi].reshape(-1), axis=0, mode="clip")
        send = send.reshape(experts_all, size * chunks, LANES)
        received = lax.all_to_all(send, ALL, split_axis=0, concat_axis=0, tiled=True)
        outputs = expert_block(received.reshape(experts_all * size, width), w_gate_up, w_down)
        outputs = outputs.reshape(experts_all, size * chunks, LANES)
        returned = lax.all_to_all(outputs, ALL, split_axis=0, concat_axis=0, tiled=True)
        returned = returned.reshape(experts_all * size, chunks, LANES)
        inside = (slots >= lo) & (slots < hi)
        picked = jnp.take(returned, chosen * size + slots - lo, axis=0, mode="clip")
        scaled = jnp.where(inside, weights, 0.0)[:, None, None] * picked.astype(jnp.float32)
        part = jnp.sum(scaled.reshape(tok_count, top_count, chunks, LANES), axis=1)
        moe_sum = part if moe_sum is None else moe_sum + part
    mixed = (residual + moe_sum.reshape(tok_count, width)).astype(jnp.bfloat16)
    return (attended, mixed)


def solution(mesh):
    n_expert = mesh.shape["expert"]
    n_tensor = mesh.shape["tensor"]
    n_core = 2 if n_tensor % 2 == 0 else 1
    n_xhi = 2 if n_expert % 32 == 0 else 1
    n_z = 4 if n_expert % 4 == 0 else 1
    shape = (n_expert // (n_xhi * n_z), n_xhi, n_z, n_tensor // n_core, n_core)
    mesh3 = Mesh(np.asarray(mesh.devices).reshape(shape), ALL)
    tensor = ("xlo", "core")
    in_specs = (
        P(ALL, None),
        P(EXPERT, tensor),
        P(tensor, EXPERT),
        P(),
        P(ALL, None),
        P(ALL, None),
        P(ALL, None, None),
        P(ALL, None, None),
    )
    out_specs = (P(ALL, None), P(ALL, None))
    return jax.shard_map(
        on_device, mesh=mesh3, in_specs=in_specs, out_specs=out_specs, check_vma=False
    )
```

```python
import jax
import jax.numpy as jnp
import numpy as np
from jax import lax
from jax.experimental import pallas as pl
from jax.experimental.pallas import tpu as pltpu
from jax.sharding import Mesh
from jax.sharding import PartitionSpec as P

LANES = 128
EXPERT = ("y", "xhi", "z")
ALL = EXPERT + ("xlo", "core")


def expert_block(received, w_gate_up, w_down):
    hidden_units = w_down.shape[1]
    gate_and_up = jnp.dot(received, w_gate_up[0], preferred_element_type=jnp.float32)
    activated = (jax.nn.silu(gate_and_up[:, :hidden_units]) * gate_and_up[:, hidden_units:]).astype(
        jnp.bfloat16
    )
    return jnp.dot(activated, w_down[0], preferred_element_type=jnp.float32).astype(jnp.bfloat16)


def ring_gather(block, axis):
    n = lax.axis_size(axis)
    me = lax.axis_index(axis)
    plus = [(i, (i + 1) % n) for i in range(n)]
    minus = [(i, (i - 1) % n) for i in range(n)]
    from_left = lax.ppermute(block, axis, perm=plus)
    from_right = lax.ppermute(block, axis, perm=minus)
    half = block.shape[-1] // 2
    far = jnp.concatenate(
        [
            lax.ppermute(from_left[..., :half], axis, perm=plus),
            lax.ppermute(from_right[..., half:], axis, perm=minus),
        ],
        axis=-1,
    )
    by_step = jnp.stack([block, from_right, far, from_left])
    order = (jnp.arange(n, dtype=jnp.int32) - me) % n
    return jnp.take(by_step, order, axis=0)


def gather_columns(w_out):
    staged = lax.all_gather(w_out, "xhi", axis=0)
    first = lax.all_gather(staged[0], "y", axis=1, tiled=True)
    first = lax.all_gather(first, "z", axis=1, tiled=True)
    second = ring_gather(staged[1], "z")
    second = ring_gather(second, "y")
    return first, second


def project(context, w_out):
    n_x = lax.axis_size("xlo")
    n_c = lax.axis_size("core")
    rows = context.shape[0] // (n_x * n_c)
    context = context.reshape(n_x, n_c, rows, -1).transpose(1, 0, 2, 3).reshape(n_x * n_c * rows, -1)
    first, second = gather_columns(w_out)
    me = lax.axis_index("xlo")

    def over_tensor(partial_sums):
        chip_sums = lax.psum_scatter(partial_sums, "core", scatter_dimension=0, tiled=True)
        chip_sums = chip_sums.reshape(n_x, rows, -1)
        own = lax.dynamic_index_in_dim(chip_sums, me, axis=0, keepdims=False)
        other = lax.dynamic_index_in_dim(chip_sums, 1 - me, axis=0, keepdims=False)
        arrived = lax.ppermute(other.astype(jnp.bfloat16), "xlo", perm=[(0, 1), (1, 0)])
        return own + arrived.astype(jnp.float32)

    by_gathers = over_tensor(jnp.dot(context, first, preferred_element_type=jnp.float32))
    other = jnp.einsum("th,yzhl->tyzl", context, second, preferred_element_type=jnp.float32)
    by_rings = over_tensor(other.reshape(other.shape[0], -1))
    n_y, n_z = lax.axis_size("y"), lax.axis_size("z")
    by_gathers = by_gathers.reshape(rows, n_z, n_y, -1).transpose(0, 2, 1, 3)
    by_rings = by_rings.reshape(rows, n_y, n_z, -1)
    return jnp.stack([by_gathers, by_rings], axis=2).reshape(rows, -1)


def on_device(hidden_in, context, w_out, norm_gain, expert_ids, route_weight, w_gate_up, w_down):
    tok_count, width = hidden_in.shape
    chunks = width // LANES
    projected = project(context, w_out)
    residual = hidden_in.astype(jnp.float32) + projected
    attended = residual.astype(jnp.bfloat16)
    inverse = lax.rsqrt(jnp.mean(residual * residual, axis=1, keepdims=True) + 1e-06)
    normed = (residual * inverse * norm_gain[None, :]).astype(jnp.bfloat16)
    top_count = expert_ids.shape[1]
    experts_all = lax.axis_size(ALL)
    capacity = tok_count * top_count * 9 // (8 * experts_all)
    rows_all = experts_all * capacity
    chosen = expert_ids.reshape(-1)
    onehot = (chosen[:, None] == jnp.arange(experts_all, dtype=jnp.int32)[None, :]).astype(
        jnp.int32
    )
    before = jnp.cumsum(onehot, axis=0) - onehot
    slots = jnp.sum(before * onehot, axis=1)
    target = chosen * capacity + slots
    token_index = jnp.arange(tok_count * top_count, dtype=jnp.int32) // top_count
    source = jnp.full((rows_all,), tok_count, jnp.int32).at[target].set(token_index)
    source = source.reshape(experts_all, capacity)
    normed3 = jnp.concatenate(
        [normed.reshape(tok_count, chunks, LANES), jnp.zeros((1, chunks, LANES), jnp.bfloat16)],
        axis=0,
    )
    weights = route_weight.reshape(-1)
    groups = 2
    bounds = [capacity * g // groups for g in range(groups + 1)]
    moe_sum = None
    for lo, hi in zip(bounds[:-1], bounds[1:]):
        size = hi - lo
        send = jnp.take(normed3, source[:, lo:hi].reshape(-1), axis=0, mode="clip")
        send = send.reshape(experts_all, size * chunks, LANES)
        received = lax.all_to_all(send, ALL, split_axis=0, concat_axis=0, tiled=True)
        outputs = expert_block(received.reshape(experts_all * size, width), w_gate_up, w_down)
        outputs = outputs.reshape(experts_all, size * chunks, LANES)
        returned = lax.all_to_all(outputs, ALL, split_axis=0, concat_axis=0, tiled=True)
        returned = returned.reshape(experts_all * size, chunks, LANES)
        inside = (slots >= lo) & (slots < hi)
        picked = jnp.take(returned, chosen * size + slots - lo, axis=0, mode="clip")
        scaled = jnp.where(inside, weights, 0.0)[:, None, None] * picked.astype(jnp.float32)
        part = jnp.sum(scaled.reshape(tok_count, top_count, chunks, LANES), axis=1)
        moe_sum = part if moe_sum is None else moe_sum + part
    mixed = (residual + moe_sum.reshape(tok_count, width)).astype(jnp.bfloat16)
    return (attended, mixed)


def solution(mesh):
    n_expert = mesh.shape["expert"]
    n_tensor = mesh.shape["tensor"]
    n_core = 2 if n_tensor % 2 == 0 else 1
    n_xhi = 2 if n_expert % 32 == 0 else 1
    n_z = 4 if n_expert % 4 == 0 else 1
    shape = (n_expert // (n_xhi * n_z), n_xhi, n_z, n_tensor // n_core, n_core)
    mesh3 = Mesh(np.asarray(mesh.devices).reshape(shape), ALL)
    tensor = ("xlo", "core")
    in_specs = (
        P(ALL, None),
        P(EXPERT, tensor),
        P(tensor, EXPERT),
        P(),
        P(ALL, None),
        P(ALL, None),
        P(ALL, None, None),
        P(ALL, None, None),
    )
    out_specs = (P(ALL, None), P(ALL, None))
    return jax.shard_map(
        on_device, mesh=mesh3, in_specs=in_specs, out_specs=out_specs, check_vma=False
    )
```

```python
import jax
import jax.numpy as jnp
import numpy as np
from jax import lax
from jax.experimental import pallas as pl
from jax.experimental.pallas import tpu as pltpu
from jax.sharding import Mesh
from jax.sharding import PartitionSpec as P

LANES = 128
EXPERT = ("y", "xhi", "z")
ALL = EXPERT + ("xlo", "core")


def expert_block(received, w_gate_up, w_down):
    hidden_units = w_down.shape[1]
    gate_and_up = jnp.dot(received, w_gate_up[0], preferred_element_type=jnp.float32)
    activated = (jax.nn.silu(gate_and_up[:, :hidden_units]) * gate_and_up[:, hidden_units:]).astype(
        jnp.bfloat16
    )
    return jnp.dot(activated, w_down[0], preferred_element_type=jnp.float32).astype(jnp.bfloat16)


def ring_gather(block, axis):
    n = lax.axis_size(axis)
    me = lax.axis_index(axis)
    plus = [(i, (i + 1) % n) for i in range(n)]
    minus = [(i, (i - 1) % n) for i in range(n)]
    from_left = lax.ppermute(block, axis, perm=plus)
    from_right = lax.ppermute(block, axis, perm=minus)
    half = block.shape[-1] // 2
    far = jnp.concatenate(
        [
            lax.ppermute(from_left[..., :half], axis, perm=plus),
            lax.ppermute(from_right[..., half:], axis, perm=minus),
        ],
        axis=-1,
    )
    by_step = jnp.stack([block, from_right, far, from_left])
    order = (jnp.arange(n, dtype=jnp.int32) - me) % n
    return jnp.take(by_step, order, axis=0)


def gather_columns(w_out):
    partner = lax.ppermute(w_out, "xhi", perm=[(0, 1), (1, 0)])
    first = lax.all_gather(w_out, "y", axis=1, tiled=True)
    first = lax.all_gather(first, "z", axis=1, tiled=True)
    second = ring_gather(partner, "z")
    second = ring_gather(second, "y")
    return first, second


def project(context, w_out):
    n_x = lax.axis_size("xlo")
    n_c = lax.axis_size("core")
    rows = context.shape[0] // (n_x * n_c)
    context = context.reshape(n_x, n_c, rows, -1).transpose(1, 0, 2, 3).reshape(n_x * n_c * rows, -1)
    first, second = gather_columns(w_out)
    me = lax.axis_index("xlo")

    def over_tensor(partial_sums):
        chip_sums = lax.psum_scatter(partial_sums, "core", scatter_dimension=0, tiled=True)
        chip_sums = chip_sums.reshape(n_x, rows, -1)
        own = lax.dynamic_index_in_dim(chip_sums, me, axis=0, keepdims=False)
        other = lax.dynamic_index_in_dim(chip_sums, 1 - me, axis=0, keepdims=False)
        arrived = lax.ppermute(other.astype(jnp.bfloat16), "xlo", perm=[(0, 1), (1, 0)])
        return own + arrived.astype(jnp.float32)

    by_gathers = over_tensor(jnp.dot(context, first, preferred_element_type=jnp.float32))
    other = jnp.einsum("th,yzhl->tyzl", context, second, preferred_element_type=jnp.float32)
    by_rings = over_tensor(other.reshape(other.shape[0], -1))
    n_y, n_z = lax.axis_size("y"), lax.axis_size("z")
    by_gathers = by_gathers.reshape(rows, n_z, n_y, -1).transpose(0, 2, 1, 3)
    by_rings = by_rings.reshape(rows, n_y, n_z, -1)
    low_first = lax.axis_index("xhi") == 0
    low = jnp.where(low_first, by_gathers, by_rings)
    high = jnp.where(low_first, by_rings, by_gathers)
    return jnp.stack([low, high], axis=2).reshape(rows, -1)


def on_device(hidden_in, context, w_out, norm_gain, expert_ids, route_weight, w_gate_up, w_down):
    tok_count, width = hidden_in.shape
    chunks = width // LANES
    projected = project(context, w_out)
    residual = hidden_in.astype(jnp.float32) + projected
    attended = residual.astype(jnp.bfloat16)
    inverse = lax.rsqrt(jnp.mean(residual * residual, axis=1, keepdims=True) + 1e-06)
    normed = (residual * inverse * norm_gain[None, :]).astype(jnp.bfloat16)
    top_count = expert_ids.shape[1]
    experts_all = lax.axis_size(ALL)
    capacity = tok_count * top_count * 9 // (8 * experts_all)
    rows_all = experts_all * capacity
    chosen = expert_ids.reshape(-1)
    onehot = (chosen[:, None] == jnp.arange(experts_all, dtype=jnp.int32)[None, :]).astype(
        jnp.int32
    )
    before = jnp.cumsum(onehot, axis=0) - onehot
    slots = jnp.sum(before * onehot, axis=1)
    target = chosen * capacity + slots
    token_index = jnp.arange(tok_count * top_count, dtype=jnp.int32) // top_count
    source = jnp.full((rows_all,), tok_count, jnp.int32).at[target].set(token_index)
    source = source.reshape(experts_all, capacity)
    normed3 = jnp.concatenate(
        [normed.reshape(tok_count, chunks, LANES), jnp.zeros((1, chunks, LANES), jnp.bfloat16)],
        axis=0,
    )
    weights = route_weight.reshape(-1)
    groups = 2
    bounds = [capacity * g // groups for g in range(groups + 1)]
    moe_sum = None
    for lo, hi in zip(bounds[:-1], bounds[1:]):
        size = hi - lo
        send = jnp.take(normed3, source[:, lo:hi].reshape(-1), axis=0, mode="clip")
        send = send.reshape(experts_all, size * chunks, LANES)
        received = lax.all_to_all(send, ALL, split_axis=0, concat_axis=0, tiled=True)
        outputs = expert_block(received.reshape(experts_all * size, width), w_gate_up, w_down)
        outputs = outputs.reshape(experts_all, size * chunks, LANES)
        returned = lax.all_to_all(outputs, ALL, split_axis=0, concat_axis=0, tiled=True)
        returned = returned.reshape(experts_all * size, chunks, LANES)
        inside = (slots >= lo) & (slots < hi)
        picked = jnp.take(returned, chosen * size + slots - lo, axis=0, mode="clip")
        scaled = jnp.where(inside, weights, 0.0)[:, None, None] * picked.astype(jnp.float32)
        part = jnp.sum(scaled.reshape(tok_count, top_count, chunks, LANES), axis=1)
        moe_sum = part if moe_sum is None else moe_sum + part
    mixed = (residual + moe_sum.reshape(tok_count, width)).astype(jnp.bfloat16)
    return (attended, mixed)


def solution(mesh):
    n_expert = mesh.shape["expert"]
    n_tensor = mesh.shape["tensor"]
    n_core = 2 if n_tensor % 2 == 0 else 1
    n_xhi = 2 if n_expert % 32 == 0 else 1
    n_z = 4 if n_expert % 4 == 0 else 1
    shape = (n_expert // (n_xhi * n_z), n_xhi, n_z, n_tensor // n_core, n_core)
    mesh3 = Mesh(np.asarray(mesh.devices).reshape(shape), ALL)
    tensor = ("xlo", "core")
    in_specs = (
        P(ALL, None),
        P(EXPERT, tensor),
        P(tensor, EXPERT),
        P(),
        P(ALL, None),
        P(ALL, None),
        P(ALL, None, None),
        P(ALL, None, None),
    )
    out_specs = (P(ALL, None), P(ALL, None))
    return jax.shard_map(
        on_device, mesh=mesh3, in_specs=in_specs, out_specs=out_specs, check_vma=False
    )
```

```python
import jax
import jax.numpy as jnp
import numpy as np
from jax import lax
from jax.experimental import pallas as pl
from jax.experimental.pallas import tpu as pltpu
from jax.sharding import Mesh
from jax.sharding import PartitionSpec as P

LANES = 128
EXPERT = ("y", "xhi", "z")
ALL = EXPERT + ("xlo", "core")


def expert_block(received, w_gate_up, w_down):
    hidden_units = w_down.shape[1]
    gate_and_up = jnp.dot(received, w_gate_up[0], preferred_element_type=jnp.float32)
    activated = (jax.nn.silu(gate_and_up[:, :hidden_units]) * gate_and_up[:, hidden_units:]).astype(
        jnp.bfloat16
    )
    return jnp.dot(activated, w_down[0], preferred_element_type=jnp.float32).astype(jnp.bfloat16)


def ring_gather(block, axis, natural=True):
    n = lax.axis_size(axis)
    me = lax.axis_index(axis)
    plus = [(i, (i + 1) % n) for i in range(n)]
    minus = [(i, (i - 1) % n) for i in range(n)]
    from_left = lax.ppermute(block, axis, perm=plus)
    from_right = lax.ppermute(block, axis, perm=minus)
    half = block.shape[-1] // 2
    far = jnp.concatenate(
        [
            lax.ppermute(from_left[..., :half], axis, perm=plus),
            lax.ppermute(from_right[..., half:], axis, perm=minus),
        ],
        axis=-1,
    )
    by_step = jnp.stack([block, from_right, far, from_left])
    if not natural:
        return by_step
    order = (jnp.arange(n, dtype=jnp.int32) - me) % n
    return jnp.take(by_step, order, axis=0)


def gather_columns(w_out):
    staged = lax.all_gather(w_out, "xhi", axis=0)
    first = lax.all_gather(staged[0], "y", axis=1, tiled=True)
    first = lax.all_gather(first, "z", axis=1, tiled=True)
    second = ring_gather(staged[1], "z")
    second = ring_gather(second, "y", natural=False)
    return first, second


def project(context, w_out):
    n_x = lax.axis_size("xlo")
    n_c = lax.axis_size("core")
    rows = context.shape[0] // (n_x * n_c)
    context = context.reshape(n_x, n_c, rows, -1).transpose(1, 0, 2, 3).reshape(n_x * n_c * rows, -1)
    first, second = gather_columns(w_out)
    me = lax.axis_index("xlo")

    def over_tensor(partial_sums):
        chip_sums = lax.psum_scatter(partial_sums, "core", scatter_dimension=0, tiled=True)
        chip_sums = chip_sums.reshape(n_x, rows, -1)
        own = lax.dynamic_index_in_dim(chip_sums, me, axis=0, keepdims=False)
        other = lax.dynamic_index_in_dim(chip_sums, 1 - me, axis=0, keepdims=False)
        arrived = lax.ppermute(other.astype(jnp.bfloat16), "xlo", perm=[(0, 1), (1, 0)])
        return own + arrived.astype(jnp.float32)

    by_gathers = over_tensor(jnp.dot(context, first, preferred_element_type=jnp.float32))
    other = jnp.einsum("th,yzhl->tyzl", context, second, preferred_element_type=jnp.float32)
    by_rings = over_tensor(other.reshape(other.shape[0], -1))
    n_y, n_z = lax.axis_size("y"), lax.axis_size("z")
    by_gathers = by_gathers.reshape(rows, n_z, n_y, -1).transpose(0, 2, 1, 3)
    by_rings = jnp.roll(by_rings.reshape(rows, n_y, n_z, -1), lax.axis_index("y"), axis=1)
    return jnp.stack([by_gathers, by_rings], axis=2).reshape(rows, -1)


def on_device(hidden_in, context, w_out, norm_gain, expert_ids, route_weight, w_gate_up, w_down):
    tok_count, width = hidden_in.shape
    chunks = width // LANES
    projected = project(context, w_out)
    residual = hidden_in.astype(jnp.float32) + projected
    attended = residual.astype(jnp.bfloat16)
    inverse = lax.rsqrt(jnp.mean(residual * residual, axis=1, keepdims=True) + 1e-06)
    normed = (residual * inverse * norm_gain[None, :]).astype(jnp.bfloat16)
    top_count = expert_ids.shape[1]
    experts_all = lax.axis_size(ALL)
    capacity = tok_count * top_count * 9 // (8 * experts_all)
    rows_all = experts_all * capacity
    chosen = expert_ids.reshape(-1)
    onehot = (chosen[:, None] == jnp.arange(experts_all, dtype=jnp.int32)[None, :]).astype(
        jnp.int32
    )
    before = jnp.cumsum(onehot, axis=0) - onehot
    slots = jnp.sum(before * onehot, axis=1)
    target = chosen * capacity + slots
    token_index = jnp.arange(tok_count * top_count, dtype=jnp.int32) // top_count
    source = jnp.full((rows_all,), tok_count, jnp.int32).at[target].set(token_index)
    source = source.reshape(experts_all, capacity)
    normed3 = jnp.concatenate(
        [normed.reshape(tok_count, chunks, LANES), jnp.zeros((1, chunks, LANES), jnp.bfloat16)],
        axis=0,
    )
    weights = route_weight.reshape(-1)
    groups = 2
    bounds = [capacity * g // groups for g in range(groups + 1)]
    moe_sum = None
    for lo, hi in zip(bounds[:-1], bounds[1:]):
        size = hi - lo
        send = jnp.take(normed3, source[:, lo:hi].reshape(-1), axis=0, mode="clip")
        send = send.reshape(experts_all, size * chunks, LANES)
        received = lax.all_to_all(send, ALL, split_axis=0, concat_axis=0, tiled=True)
        outputs = expert_block(received.reshape(experts_all * size, width), w_gate_up, w_down)
        outputs = outputs.reshape(experts_all, size * chunks, LANES)
        returned = lax.all_to_all(outputs, ALL, split_axis=0, concat_axis=0, tiled=True)
        returned = returned.reshape(experts_all * size, chunks, LANES)
        inside = (slots >= lo) & (slots < hi)
        picked = jnp.take(returned, chosen * size + slots - lo, axis=0, mode="clip")
        scaled = jnp.where(inside, weights, 0.0)[:, None, None] * picked.astype(jnp.float32)
        part = jnp.sum(scaled.reshape(tok_count, top_count, chunks, LANES), axis=1)
        moe_sum = part if moe_sum is None else moe_sum + part
    mixed = (residual + moe_sum.reshape(tok_count, width)).astype(jnp.bfloat16)
    return (attended, mixed)


def solution(mesh):
    n_expert = mesh.shape["expert"]
    n_tensor = mesh.shape["tensor"]
    n_core = 2 if n_tensor % 2 == 0 else 1
    n_xhi = 2 if n_expert % 32 == 0 else 1
    n_z = 4 if n_expert % 4 == 0 else 1
    shape = (n_expert // (n_xhi * n_z), n_xhi, n_z, n_tensor // n_core, n_core)
    mesh3 = Mesh(np.asarray(mesh.devices).reshape(shape), ALL)
    tensor = ("xlo", "core")
    in_specs = (
        P(ALL, None),
        P(EXPERT, tensor),
        P(tensor, EXPERT),
        P(),
        P(ALL, None),
        P(ALL, None),
        P(ALL, None, None),
        P(ALL, None, None),
    )
    out_specs = (P(ALL, None), P(ALL, None))
    return jax.shard_map(
        on_device, mesh=mesh3, in_specs=in_specs, out_specs=out_specs, check_vma=False
    )
```

```python
import jax
import jax.numpy as jnp
import numpy as np
from jax import lax
from jax.experimental import pallas as pl
from jax.experimental.pallas import tpu as pltpu
from jax.sharding import Mesh
from jax.sharding import PartitionSpec as P

LANES = 128
EXPERT = ("y", "xhi", "z")
ALL = EXPERT + ("xlo", "core")


def expert_block(received, w_gate_up, w_down):
    hidden_units = w_down.shape[1]
    gate_and_up = jnp.dot(received, w_gate_up[0], preferred_element_type=jnp.float32)
    activated = (jax.nn.silu(gate_and_up[:, :hidden_units]) * gate_and_up[:, hidden_units:]).astype(
        jnp.bfloat16
    )
    return jnp.dot(activated, w_down[0], preferred_element_type=jnp.float32).astype(jnp.bfloat16)


def ring_gather(block, axis, natural=True):
    n = lax.axis_size(axis)
    me = lax.axis_index(axis)
    plus = [(i, (i + 1) % n) for i in range(n)]
    minus = [(i, (i - 1) % n) for i in range(n)]
    from_left = lax.ppermute(block, axis, perm=plus)
    from_right = lax.ppermute(block, axis, perm=minus)
    half = block.shape[-1] // 2
    far = jnp.concatenate(
        [
            lax.ppermute(from_left[..., :half], axis, perm=plus),
            lax.ppermute(from_right[..., half:], axis, perm=minus),
        ],
        axis=-1,
    )
    by_step = jnp.stack([block, from_right, far, from_left])
    if not natural:
        return by_step
    order = (jnp.arange(n, dtype=jnp.int32) - me) % n
    return jnp.take(by_step, order, axis=0)


def gather_columns(w_out):
    staged = lax.all_gather(w_out, "xhi", axis=0)
    first = lax.all_gather(staged[0], "y", axis=1, tiled=True)
    first = lax.all_gather(first, "z", axis=1, tiled=True)
    second = ring_gather(staged[1], "z", natural=False)
    second = ring_gather(second, "y", natural=False)
    return first, second


def project(context, w_out):
    n_x = lax.axis_size("xlo")
    n_c = lax.axis_size("core")
    rows = context.shape[0] // (n_x * n_c)
    context = context.reshape(n_x, n_c, rows, -1).transpose(1, 0, 2, 3).reshape(n_x * n_c * rows, -1)
    first, second = gather_columns(w_out)
    me = lax.axis_index("xlo")

    def over_tensor(partial_sums):
        chip_sums = lax.psum_scatter(partial_sums, "core", scatter_dimension=0, tiled=True)
        chip_sums = chip_sums.reshape(n_x, rows, -1)
        own = lax.dynamic_index_in_dim(chip_sums, me, axis=0, keepdims=False)
        other = lax.dynamic_index_in_dim(chip_sums, 1 - me, axis=0, keepdims=False)
        arrived = lax.ppermute(other.astype(jnp.bfloat16), "xlo", perm=[(0, 1), (1, 0)])
        return own + arrived.astype(jnp.float32)

    by_gathers = over_tensor(jnp.dot(context, first, preferred_element_type=jnp.float32))
    other = jnp.einsum("th,yzhl->tyzl", context, second, preferred_element_type=jnp.float32)
    by_rings = over_tensor(other.reshape(other.shape[0], -1))
    n_y, n_z = lax.axis_size("y"), lax.axis_size("z")
    by_gathers = by_gathers.reshape(rows, n_z, n_y, -1).transpose(0, 2, 1, 3)
    by_rings = jnp.roll(by_rings.reshape(rows, n_y, n_z, -1), lax.axis_index("y"), axis=1)
    by_rings = jnp.roll(by_rings, lax.axis_index("z"), axis=2)
    return jnp.stack([by_gathers, by_rings], axis=2).reshape(rows, -1)


def on_device(hidden_in, context, w_out, norm_gain, expert_ids, route_weight, w_gate_up, w_down):
    tok_count, width = hidden_in.shape
    chunks = width // LANES
    projected = project(context, w_out)
    residual = hidden_in.astype(jnp.float32) + projected
    attended = residual.astype(jnp.bfloat16)
    inverse = lax.rsqrt(jnp.mean(residual * residual, axis=1, keepdims=True) + 1e-06)
    normed = (residual * inverse * norm_gain[None, :]).astype(jnp.bfloat16)
    top_count = expert_ids.shape[1]
    experts_all = lax.axis_size(ALL)
    capacity = tok_count * top_count * 9 // (8 * experts_all)
    rows_all = experts_all * capacity
    chosen = expert_ids.reshape(-1)
    onehot = (chosen[:, None] == jnp.arange(experts_all, dtype=jnp.int32)[None, :]).astype(
        jnp.int32
    )
    before = jnp.cumsum(onehot, axis=0) - onehot
    slots = jnp.sum(before * onehot, axis=1)
    target = chosen * capacity + slots
    token_index = jnp.arange(tok_count * top_count, dtype=jnp.int32) // top_count
    source = jnp.full((rows_all,), tok_count, jnp.int32).at[target].set(token_index)
    source = source.reshape(experts_all, capacity)
    normed3 = jnp.concatenate(
        [normed.reshape(tok_count, chunks, LANES), jnp.zeros((1, chunks, LANES), jnp.bfloat16)],
        axis=0,
    )
    weights = route_weight.reshape(-1)
    groups = 2
    bounds = [capacity * g // groups for g in range(groups + 1)]
    moe_sum = None
    for lo, hi in zip(bounds[:-1], bounds[1:]):
        size = hi - lo
        send = jnp.take(normed3, source[:, lo:hi].reshape(-1), axis=0, mode="clip")
        send = send.reshape(experts_all, size * chunks, LANES)
        received = lax.all_to_all(send, ALL, split_axis=0, concat_axis=0, tiled=True)
        outputs = expert_block(received.reshape(experts_all * size, width), w_gate_up, w_down)
        outputs = outputs.reshape(experts_all, size * chunks, LANES)
        returned = lax.all_to_all(outputs, ALL, split_axis=0, concat_axis=0, tiled=True)
        returned = returned.reshape(experts_all * size, chunks, LANES)
        inside = (slots >= lo) & (slots < hi)
        picked = jnp.take(returned, chosen * size + slots - lo, axis=0, mode="clip")
        scaled = jnp.where(inside, weights, 0.0)[:, None, None] * picked.astype(jnp.float32)
        part = jnp.sum(scaled.reshape(tok_count, top_count, chunks, LANES), axis=1)
        moe_sum = part if moe_sum is None else moe_sum + part
    mixed = (residual + moe_sum.reshape(tok_count, width)).astype(jnp.bfloat16)
    return (attended, mixed)


def solution(mesh):
    n_expert = mesh.shape["expert"]
    n_tensor = mesh.shape["tensor"]
    n_core = 2 if n_tensor % 2 == 0 else 1
    n_xhi = 2 if n_expert % 32 == 0 else 1
    n_z = 4 if n_expert % 4 == 0 else 1
    shape = (n_expert // (n_xhi * n_z), n_xhi, n_z, n_tensor // n_core, n_core)
    mesh3 = Mesh(np.asarray(mesh.devices).reshape(shape), ALL)
    tensor = ("xlo", "core")
    in_specs = (
        P(ALL, None),
        P(EXPERT, tensor),
        P(tensor, EXPERT),
        P(),
        P(ALL, None),
        P(ALL, None),
        P(ALL, None, None),
        P(ALL, None, None),
    )
    out_specs = (P(ALL, None), P(ALL, None))
    return jax.shard_map(
        on_device, mesh=mesh3, in_specs=in_specs, out_specs=out_specs, check_vma=False
    )
```

```python
import jax
import jax.numpy as jnp
import numpy as np
from jax import lax
from jax.experimental import pallas as pl
from jax.experimental.pallas import tpu as pltpu
from jax.sharding import Mesh
from jax.sharding import PartitionSpec as P

LANES = 128
EXPERT = ("y", "xhi", "z")
ALL = EXPERT + ("xlo", "core")


def expert_block(received, w_gate_up, w_down):
    hidden_units = w_down.shape[1]
    gate_and_up = jnp.dot(received, w_gate_up[0], preferred_element_type=jnp.float32)
    activated = (jax.nn.silu(gate_and_up[:, :hidden_units]) * gate_and_up[:, hidden_units:]).astype(
        jnp.bfloat16
    )
    return jnp.dot(activated, w_down[0], preferred_element_type=jnp.float32).astype(jnp.bfloat16)


def ring_gather(block, axis, natural=True):
    n = lax.axis_size(axis)
    me = lax.axis_index(axis)
    plus = [(i, (i + 1) % n) for i in range(n)]
    minus = [(i, (i - 1) % n) for i in range(n)]
    from_left = lax.ppermute(block, axis, perm=plus)
    from_right = lax.ppermute(block, axis, perm=minus)
    half = block.shape[-1] // 2
    far = jnp.concatenate(
        [
            lax.ppermute(from_left[..., :half], axis, perm=plus),
            lax.ppermute(from_right[..., half:], axis, perm=minus),
        ],
        axis=-1,
    )
    by_step = jnp.stack([block, from_right, far, from_left])
    if not natural:
        return by_step
    order = (jnp.arange(n, dtype=jnp.int32) - me) % n
    return jnp.take(by_step, order, axis=0)


def gather_columns(w_out):
    staged = lax.all_gather(w_out, "xhi", axis=0)
    first = lax.all_gather(staged[0], "y", axis=1, tiled=True)
    first = lax.all_gather(first, "z", axis=1, tiled=True)
    second = ring_gather(staged[1], "z", natural=False)
    second = ring_gather(second, "y", natural=False)
    return first, second


def project(context, w_out):
    n_x = lax.axis_size("xlo")
    n_c = lax.axis_size("core")
    rows = context.shape[0] // (n_x * n_c)
    context = context.reshape(n_x, n_c, rows, -1).transpose(1, 0, 2, 3).reshape(n_x * n_c * rows, -1)
    first, second = gather_columns(w_out)
    me = lax.axis_index("xlo")

    def over_tensor(partial_sums):
        chip_sums = lax.psum_scatter(partial_sums, "core", scatter_dimension=0, tiled=True)
        chip_sums = chip_sums.reshape(n_x, rows, -1)
        own = lax.dynamic_index_in_dim(chip_sums, me, axis=0, keepdims=False)
        other = lax.dynamic_index_in_dim(chip_sums, 1 - me, axis=0, keepdims=False)
        arrived = lax.ppermute(other.astype(jnp.bfloat16), "xlo", perm=[(0, 1), (1, 0)])
        return own + arrived.astype(jnp.float32)

    by_gathers = over_tensor(jnp.dot(context, first, preferred_element_type=jnp.float32))
    other = jnp.einsum("th,yzhl->tyzl", context, second, preferred_element_type=jnp.float32)
    by_rings = over_tensor(other.reshape(other.shape[0], -1))
    n_y, n_z = lax.axis_size("y"), lax.axis_size("z")
    by_gathers = by_gathers.reshape(rows, n_z, n_y, -1).transpose(0, 2, 1, 3)
    by_rings = jnp.roll(by_rings.reshape(rows, n_y, n_z, -1), lax.axis_index("y"), axis=1)
    by_rings = jnp.roll(by_rings, lax.axis_index("z"), axis=2)
    return jnp.stack([by_gathers, by_rings], axis=2).reshape(rows, -1)


def on_device(hidden_in, context, w_out, norm_gain, expert_ids, route_weight, w_gate_up, w_down):
    tok_count, width = hidden_in.shape
    chunks = width // LANES
    projected = project(context, w_out)
    residual = hidden_in.astype(jnp.float32) + projected
    attended = residual.astype(jnp.bfloat16)
    inverse = lax.rsqrt(jnp.mean(residual * residual, axis=1, keepdims=True) + 1e-06)
    normed = (residual * inverse * norm_gain[None, :]).astype(jnp.bfloat16)
    top_count = expert_ids.shape[1]
    experts_all = lax.axis_size(ALL)
    capacity = tok_count * top_count * 9 // (8 * experts_all)
    rows_all = experts_all * capacity
    chosen = expert_ids.reshape(-1)
    onehot = (chosen[:, None] == jnp.arange(experts_all, dtype=jnp.int32)[None, :]).astype(
        jnp.int32
    )
    before = jnp.cumsum(onehot, axis=0) - onehot
    slots = jnp.sum(before * onehot, axis=1)
    target = chosen * capacity + slots
    token_index = jnp.arange(tok_count * top_count, dtype=jnp.int32) // top_count
    source = jnp.full((rows_all,), tok_count, jnp.int32).at[target].set(token_index)
    source = source.reshape(experts_all, capacity)
    normed3 = jnp.concatenate(
        [normed.reshape(tok_count, chunks, LANES), jnp.zeros((1, chunks, LANES), jnp.bfloat16)],
        axis=0,
    )
    weights = route_weight.reshape(-1)
    groups = 2
    bounds = [-(-capacity * g // groups) for g in range(groups + 1)]
    moe_sum = None
    for lo, hi in zip(bounds[:-1], bounds[1:]):
        size = hi - lo
        send = jnp.take(normed3, source[:, lo:hi].reshape(-1), axis=0, mode="clip")
        send = send.reshape(experts_all, size * chunks, LANES)
        received = lax.all_to_all(send, ALL, split_axis=0, concat_axis=0, tiled=True)
        outputs = expert_block(received.reshape(experts_all * size, width), w_gate_up, w_down)
        outputs = outputs.reshape(experts_all, size * chunks, LANES)
        returned = lax.all_to_all(outputs, ALL, split_axis=0, concat_axis=0, tiled=True)
        returned = returned.reshape(experts_all * size, chunks, LANES)
        inside = (slots >= lo) & (slots < hi)
        picked = jnp.take(returned, chosen * size + slots - lo, axis=0, mode="clip")
        scaled = jnp.where(inside, weights, 0.0)[:, None, None] * picked.astype(jnp.float32)
        part = jnp.sum(scaled.reshape(tok_count, top_count, chunks, LANES), axis=1)
        moe_sum = part if moe_sum is None else moe_sum + part
    mixed = (residual + moe_sum.reshape(tok_count, width)).astype(jnp.bfloat16)
    return (attended, mixed)


def solution(mesh):
    n_expert = mesh.shape["expert"]
    n_tensor = mesh.shape["tensor"]
    n_core = 2 if n_tensor % 2 == 0 else 1
    n_xhi = 2 if n_expert % 32 == 0 else 1
    n_z = 4 if n_expert % 4 == 0 else 1
    shape = (n_expert // (n_xhi * n_z), n_xhi, n_z, n_tensor // n_core, n_core)
    mesh3 = Mesh(np.asarray(mesh.devices).reshape(shape), ALL)
    tensor = ("xlo", "core")
    in_specs = (
        P(ALL, None),
        P(EXPERT, tensor),
        P(tensor, EXPERT),
        P(),
        P(ALL, None),
        P(ALL, None),
        P(ALL, None, None),
        P(ALL, None, None),
    )
    out_specs = (P(ALL, None), P(ALL, None))
    return jax.shard_map(
        on_device, mesh=mesh3, in_specs=in_specs, out_specs=out_specs, check_vma=False
    )
```

```python
import jax
import jax.numpy as jnp
import numpy as np
from jax import lax
from jax.experimental import pallas as pl
from jax.experimental.pallas import tpu as pltpu
from jax.sharding import Mesh
from jax.sharding import PartitionSpec as P

LANES = 128
EXPERT = ("y", "xhi", "z")
ALL = EXPERT + ("xlo", "core")


def expert_block(received, w_gate_up, w_down):
    hidden_units = w_down.shape[1]
    gate_and_up = jnp.dot(received, w_gate_up[0], preferred_element_type=jnp.float32)
    activated = (jax.nn.silu(gate_and_up[:, :hidden_units]) * gate_and_up[:, hidden_units:]).astype(
        jnp.bfloat16
    )
    return jnp.dot(activated, w_down[0], preferred_element_type=jnp.float32).astype(jnp.bfloat16)


def ring_gather(block, axis, natural=True):
    n = lax.axis_size(axis)
    me = lax.axis_index(axis)
    plus = [(i, (i + 1) % n) for i in range(n)]
    minus = [(i, (i - 1) % n) for i in range(n)]
    from_left = lax.ppermute(block, axis, perm=plus)
    from_right = lax.ppermute(block, axis, perm=minus)
    half = block.shape[-1] // 2
    far = jnp.concatenate(
        [
            lax.ppermute(from_left[..., :half], axis, perm=plus),
            lax.ppermute(from_right[..., half:], axis, perm=minus),
        ],
        axis=-1,
    )
    by_step = jnp.stack([block, from_right, far, from_left])
    if not natural:
        return by_step
    order = (jnp.arange(n, dtype=jnp.int32) - me) % n
    return jnp.take(by_step, order, axis=0)


def gather_columns(w_out):
    staged = lax.all_gather(w_out, "xhi", axis=0)
    first = lax.all_gather(staged[0], "y", axis=1, tiled=True)
    first = lax.all_gather(first, "z", axis=1, tiled=True)
    second = ring_gather(staged[1], "z", natural=False)
    second = ring_gather(second, "y", natural=False)
    return first, second


def project(context, w_out):
    n_x = lax.axis_size("xlo")
    n_c = lax.axis_size("core")
    rows = context.shape[0] // (n_x * n_c)
    context = context.reshape(n_x, n_c, rows, -1).transpose(1, 0, 2, 3).reshape(n_x * n_c * rows, -1)
    first, second = gather_columns(w_out)
    me = lax.axis_index("xlo")

    def over_tensor(partial_sums):
        chip_sums = lax.psum_scatter(partial_sums, "core", scatter_dimension=0, tiled=True)
        chip_sums = chip_sums.reshape(n_x, rows, -1)
        own = lax.dynamic_index_in_dim(chip_sums, me, axis=0, keepdims=False)
        other = lax.dynamic_index_in_dim(chip_sums, 1 - me, axis=0, keepdims=False)
        arrived = lax.ppermute(other.astype(jnp.bfloat16), "xlo", perm=[(0, 1), (1, 0)])
        return own + arrived.astype(jnp.float32)

    by_gathers = over_tensor(jnp.dot(context, first, preferred_element_type=jnp.float32))
    other = jnp.einsum("th,yzhl->tyzl", context, second, preferred_element_type=jnp.float32)
    by_rings = over_tensor(other.reshape(other.shape[0], -1))
    n_y, n_z = lax.axis_size("y"), lax.axis_size("z")
    by_gathers = by_gathers.reshape(rows, n_z, n_y, -1).transpose(0, 2, 1, 3)
    by_rings = jnp.roll(by_rings.reshape(rows, n_y, n_z, -1), lax.axis_index("y"), axis=1)
    by_rings = jnp.roll(by_rings, lax.axis_index("z"), axis=2)
    return jnp.stack([by_gathers, by_rings], axis=2).reshape(rows, -1)


def on_device(hidden_in, context, w_out, norm_gain, expert_ids, route_weight, w_gate_up, w_down):
    tok_count, width = hidden_in.shape
    chunks = width // LANES
    projected = project(context, w_out)
    residual = hidden_in.astype(jnp.float32) + projected
    attended = residual.astype(jnp.bfloat16)
    inverse = lax.rsqrt(jnp.mean(residual * residual, axis=1, keepdims=True) + 1e-06)
    normed = (residual * inverse * norm_gain[None, :]).astype(jnp.bfloat16)
    top_count = expert_ids.shape[1]
    experts_all = lax.axis_size(ALL)
    capacity = tok_count * top_count * 9 // (8 * experts_all)
    rows_all = experts_all * capacity
    chosen = expert_ids.reshape(-1)
    onehot = (chosen[:, None] == jnp.arange(experts_all, dtype=jnp.int32)[None, :]).astype(
        jnp.int32
    )
    before = jnp.cumsum(onehot, axis=0) - onehot
    slots = jnp.sum(before * onehot, axis=1)
    target = chosen * capacity + slots
    token_index = jnp.arange(tok_count * top_count, dtype=jnp.int32) // top_count
    source = jnp.full((rows_all,), tok_count, jnp.int32).at[target].set(token_index)
    source = source.reshape(experts_all, capacity)
    normed3 = jnp.concatenate(
        [normed.reshape(tok_count, chunks, LANES), jnp.zeros((1, chunks, LANES), jnp.bfloat16)],
        axis=0,
    )
    weights = route_weight.reshape(-1)
    groups = 2
    bounds = [-(-capacity * g // groups) for g in range(groups + 1)]
    moe_sum = None
    for lo, hi in zip(bounds[:-1], bounds[1:]):
        size = hi - lo
        send = normed3.at[source[:, lo:hi].reshape(-1)].get(mode="promise_in_bounds")
        send = send.reshape(experts_all, size * chunks, LANES)
        received = lax.all_to_all(send, ALL, split_axis=0, concat_axis=0, tiled=True)
        outputs = expert_block(received.reshape(experts_all * size, width), w_gate_up, w_down)
        outputs = outputs.reshape(experts_all, size * chunks, LANES)
        returned = lax.all_to_all(outputs, ALL, split_axis=0, concat_axis=0, tiled=True)
        returned = returned.reshape(experts_all * size, chunks, LANES)
        inside = (slots >= lo) & (slots < hi)
        picked = jnp.take(returned, chosen * size + slots - lo, axis=0, mode="clip")
        scaled = jnp.where(inside, weights, 0.0)[:, None, None] * picked.astype(jnp.float32)
        part = jnp.sum(scaled.reshape(tok_count, top_count, chunks, LANES), axis=1)
        moe_sum = part if moe_sum is None else moe_sum + part
    mixed = (residual + moe_sum.reshape(tok_count, width)).astype(jnp.bfloat16)
    return (attended, mixed)


def solution(mesh):
    n_expert = mesh.shape["expert"]
    n_tensor = mesh.shape["tensor"]
    n_core = 2 if n_tensor % 2 == 0 else 1
    n_xhi = 2 if n_expert % 32 == 0 else 1
    n_z = 4 if n_expert % 4 == 0 else 1
    shape = (n_expert // (n_xhi * n_z), n_xhi, n_z, n_tensor // n_core, n_core)
    mesh3 = Mesh(np.asarray(mesh.devices).reshape(shape), ALL)
    tensor = ("xlo", "core")
    in_specs = (
        P(ALL, None),
        P(EXPERT, tensor),
        P(tensor, EXPERT),
        P(),
        P(ALL, None),
        P(ALL, None),
        P(ALL, None, None),
        P(ALL, None, None),
    )
    out_specs = (P(ALL, None), P(ALL, None))
    return jax.shard_map(
        on_device, mesh=mesh3, in_specs=in_specs, out_specs=out_specs, check_vma=False
    )
```
